128 devices in a mesh: gx: 8 (over z, core), gy: 16 (over y, x).
Axes of the slice: x: 4, y: 4, z: 4, core: 2. Of those that a mesh axis runs over, the one named last changes fastest.
Arguments:
- water_depth: float32 [512, 4096], P('gx', 'gy'), may hold values from 0.2 to 4
- bed_level: float32 [512, 4096], P('gx', 'gy'), may hold values from -1.2 to 1.2
- roughness: float32 [512, 4096], P('gx', 'gy'), may hold values from 0.03 to 0.15
- wet_mask: int32 [512, 4096], P('gx', 'gy'), may hold values 0 or 1
- flux_east: float32 [512, 4096], P('gx', 'gy'), may hold values from -3 to 3
- flux_south: float32 [512, 4096], P('gx', 'gy'), may hold values from -3 to 3
- bank_row: int32 [4194304], P(('gx', 'gy')), may hold values from 0 to 63
- bank_column: int32 [4194304], P(('gx', 'gy')), may hold values from 0 to 255
- link_section: int32 [4194304], P(('gx', 'gy')), may hold values from 0 to 31
- link_reach: int32 [4194304], P(('gx', 'gy')), may hold values from 0 to 511
- link_crest: float32 [4194304], P(('gx', 'gy')), may hold values from 0.5 to 3
- link_factor: float32 [4194304], P(('gx', 'gy')), may hold values from 0.2 to 1
- link_regime: int32 [4194304], P(('gx', 'gy')), may hold values from 0 to 2
- channel_segment: float32 [4096, 512], P(('gx', 'gy')), may hold values from -1 to 5.2
- old_discharge: float32 [4096, 512], P(('gx', 'gy')), may hold values from -6 to 6
- courant: float32 [4096, 512], P(('gx', 'gy')), may hold values from 30 to 6144000
- junction: int32 [4096, 512], P(('gx', 'gy')), may hold values 0 or 1
- pass_share: float32 [4096, 512], P(('gx', 'gy')), may hold values from 0.5 to 0.8
- inflow: float32 [512], replicated, may hold values from -5 to 5
Outputs:
- new_depth: float32 [512, 4096], P('gx', 'gy')
- new_flux_east: float32 [512, 4096], P('gx', 'gy')
- new_flux_south: float32 [512, 4096], P('gx', 'gy')
- new_discharge: float32 [4096, 512], P(('gx', 'gy'))
The draws below stay inside these ranges and needn't reach their ends.
All inputs are finite; a program needn't handle non-finite values. No bound on the sum of `wet_mask` or of `junction` on one device may be relied on, other than what follows from the above.
Results may differ from the reference program's by a relative error of at most 0.00029.
Values sent between devices are 32-bit elements; how exact they have to be, the bound alone decides.
A program may use at most 64 MiB of HBM per device.

```python
import math
import jax
import jax.numpy as jnp
from jax import lax

CX = 64
CY = 256
SUBSTEPS = 4
SEC_DEV = 32
RIV = 512
BANK_DEV = 32768
NX = 512
NY = 4096
SECTIONS = 4096
LINKS = 4194304
N_GX = 8
N_GY = 16


def bed_law(key, shape):
    return jnp.clip(0.3 * jax.random.normal(key, shape, jnp.float32), -1.2, 1.2)


def depth_law(key, shape):
    return jnp.exp(jax.random.uniform(key, shape, jnp.float32, math.log(0.2), math.log(4.0)))


def draw_water_depth(key, part):
    return depth_law(jax.random.fold_in(key, 2), (NX, NY))


def draw_bed_level(key, part):
    return bed_law(jax.random.fold_in(key, 1), (NX, NY))


def draw_channel_segment(key, part):
    return bed_law(jax.random.fold_in(key, 3), (SECTIONS, RIV)) + depth_law(jax.random.fold_in(key, 4), (SECTIONS, RIV))


def draw_courant(key, part):
    lane_key = jax.random.fold_in(key, 11)
    block_key = jax.random.fold_in(key, 12)
    cell_key = jax.random.fold_in(key, 13)
    lowest = jnp.float32(math.log(150.0))
    highest = math.log(1000.0) + jnp.log(jnp.float32(SECTIONS))
    lane = jnp.exp(lowest + (highest - lowest) * jax.random.uniform(lane_key, (1, RIV), jnp.float32))
    blocks = jnp.exp(jax.random.uniform(block_key, (SECTIONS // SEC_DEV, 1), jnp.float32, math.log(0.5), math.log(1.5)))
    blocks = jnp.repeat(blocks, SEC_DEV, axis=0)
    rough = jax.random.uniform(cell_key, (SECTIONS, RIV), jnp.float32, 0.5, 1.0)
    return lane * blocks * rough


def touch_ends(result, rng, smallest, largest):
    longest = result.shape.index(max(result.shape))
    spots = []
    for shift in (0, 1):
        where = [jax.random.randint(jax.random.fold_in(rng, axis), (), 0, length) for axis, length in enumerate(result.shape)]
        where[longest] = (where[longest] + shift) % result.shape[longest]
        spots.append(tuple(where))
    return result.at[spots[0]].set(smallest).at[spots[1]].set(largest)


def block_scale(key, extent, shards, least, top_value):
    def one(axis_at, blocks):
        draws = jax.random.uniform(jax.random.fold_in(jax.random.fold_in(key, 6), axis_at), (blocks,), jnp.float32, least / len(shards), top_value / len(shards))
        return jnp.repeat(jnp.exp(draws), extent[axis_at] // blocks).reshape((-1,) + (1,) * (len(extent) - axis_at - 1))

    level = one(*shards[0])
    for cut in shards[1:]:
        level = level * one(*cut)
    return level


def scatter_about(rng, dims, deviation, most, cuts=(), kind=jnp.bfloat16):
    array = deviation * jax.random.normal(rng, dims, jnp.float32)
    if cuts:
        array = array * block_scale(rng, dims, cuts, -0.22, 0.18)
    return jnp.clip(array, -most, most).astype(kind)


def setup_inputs(seed: int = 0) -> dict:
    key_list = jax.random.split(jax.random.key(seed), 20)
    return {
        "water_depth": draw_water_depth(jax.random.fold_in(key_list[19], 71), 0),
        "bed_level": draw_bed_level(jax.random.fold_in(key_list[19], 71), 0),
        "roughness": jnp.clip(jnp.exp(math.log(0.15) - 1.609438 * jax.random.uniform(key_list[2], (NX, NY), jnp.float32) ** block_scale(key_list[2], (NX, NY), ((0, 8), (1, 16)), -0.2, 0.2)), 0.03, 0.15),
        "wet_mask": touch_ends((jax.random.randint(key_list[3], (NX, NY), 0, 5) < 4).astype(jnp.int32), jax.random.fold_in(key_list[3], 1), 0, 1),
        "flux_east": scatter_about(key_list[4], (NX, NY), 0.5, 3.0, ((0, 8), (1, 16)), jnp.float32),
        "flux_south": scatter_about(key_list[5], (NX, NY), 0.5, 3.0, ((0, 8), (1, 16)), jnp.float32),
        "bank_row": touch_ends(jax.random.randint(key_list[6], (LINKS,), 0, CX), jax.random.fold_in(key_list[6], 1), 0, CX - 1).astype(jnp.int32),
        "bank_column": touch_ends(jax.random.randint(key_list[7], (LINKS,), 0, CY), jax.random.fold_in(key_list[7], 1), 0, CY - 1).astype(jnp.int32),
        "link_section": touch_ends(jax.random.randint(key_list[8], (LINKS,), 0, SEC_DEV), jax.random.fold_in(key_list[8], 1), 0, SEC_DEV - 1).astype(jnp.int32),
        "link_reach": touch_ends(jax.random.randint(key_list[9], (LINKS,), 0, RIV), jax.random.fold_in(key_list[9], 1), 0, RIV - 1).astype(jnp.int32),
        "link_crest": jnp.clip(0.5 + 2.5 * jax.random.uniform(key_list[10], (LINKS,), jnp.float32) ** block_scale(key_list[10], (LINKS,), ((0, 128),), -0.2, 0.2), 0.5, 3.0),
        "link_factor": jnp.clip(jnp.exp(math.log(1.0) - 1.609438 * jax.random.uniform(key_list[11], (LINKS,), jnp.float32) ** block_scale(key_list[11], (LINKS,), ((0, 128),), -0.2, 0.2)), 0.2, 1.0),
        "link_regime": touch_ends(jax.random.randint(key_list[12], (LINKS,), 0, 3), jax.random.fold_in(key_list[12], 1), 0, 2).astype(jnp.int32),
        "channel_segment": draw_channel_segment(jax.random.fold_in(key_list[19], 71), 0),
        "old_discharge": scatter_about(key_list[14], (SECTIONS, RIV), 1.0, 6.0, ((0, 128),), jnp.float32),
        "courant": draw_courant(jax.random.fold_in(key_list[19], 71), 0),
        "junction": touch_ends((jax.random.randint(key_list[16], (SECTIONS, RIV), 0, SECTIONS) < 2).astype(jnp.int32), jax.random.fold_in(key_list[16], 1), 0, 1),
        "pass_share": jnp.clip(0.5 + 0.3 * jax.random.uniform(key_list[17], (SECTIONS, RIV), jnp.float32) ** block_scale(key_list[17], (SECTIONS, RIV), ((0, 128),), -0.2, 0.2), 0.5, 0.8),
        "inflow": scatter_about(key_list[18], (RIV,), 1.0, 5.0, (), jnp.float32),
    }


GRAVITY = 9.81
SPACING = 20.0
TIME_STEP = 2.2
MIN_FLOW_DEPTH = 0.3
IMPLICIT_WEIGHT = 0.6
LATERAL_SCALE = 0.01
BANK_GAIN = 0.5

def face_update(surface_near, surface_far, bed_near, bed_far, rough_near, rough_far, wet_near, wet_far, flux_old):
    flow_depth = jnp.maximum(jnp.maximum(surface_near, surface_far) - jnp.maximum(bed_near, bed_far), MIN_FLOW_DEPTH)
    manning = 0.5 * (rough_near + rough_far)
    slope = (surface_far - surface_near) / SPACING
    friction = 1.0 + GRAVITY * TIME_STEP * manning * manning * jnp.abs(flux_old) / jnp.power(flow_depth, 7.0 / 3.0)
    return wet_near * wet_far * (flux_old - GRAVITY * TIME_STEP * flow_depth * slope) / friction

def substep(water, east, south, bed, rough, wetness):
    surface = bed + water
    east_new = face_update(surface[:, :-1], surface[:, 1:], bed[:, :-1], bed[:, 1:], rough[:, :-1], rough[:, 1:], wetness[:, :-1], wetness[:, 1:], east[:, :-1])
    south_new = face_update(surface[:-1], surface[1:], bed[:-1], bed[1:], rough[:-1], rough[1:], wetness[:-1], wetness[1:], south[:-1])
    inner = water[1:-1, 1:-1] + TIME_STEP / SPACING * (east_new[1:-1, :-1] - east_new[1:-1, 1:] + south_new[:-1, 1:-1] - south_new[1:, 1:-1])
    return (inner, east_new[1:-1, 1:], south_new[1:, 1:-1])

def weir_flow(channel_level, plain_level, crest, factor, regime):
    upper = jnp.maximum(channel_level - crest, 0.0)
    lower = jnp.maximum(plain_level - crest, 0.0)
    free_flow = upper * jnp.sqrt(upper) - lower * jnp.sqrt(lower)
    drop = channel_level - plain_level
    drowned = drop * jnp.sqrt(jnp.abs(drop))
    return factor * jnp.where(regime == 1, free_flow, jnp.where(regime == 2, drowned, 0.0 * drop))

def reference(water_depth, bed_level, roughness, wet_mask, flux_east, flux_south, bank_row, bank_column, link_section, link_reach, link_crest, link_factor, link_regime, channel_segment, old_discharge, courant, junction, pass_share, inflow):
    devices = N_GX * N_GY
    capacity = BANK_DEV // devices
    source = jnp.arange(devices, dtype=jnp.int32)[:, None, None]
    row_index = source // N_GY * CX + bank_row.reshape(devices, devices, capacity)
    col_index = source % N_GY * CY + bank_column.reshape(devices, devices, capacity)
    plain_level = (bed_level + water_depth)[row_index, col_index]
    sections = jnp.transpose(link_section.reshape(devices, devices, capacity), (1, 0, 2))
    reaches = jnp.transpose(link_reach.reshape(devices, devices, capacity), (1, 0, 2))
    crest = jnp.transpose(link_crest.reshape(devices, devices, capacity), (1, 0, 2))
    factor = jnp.transpose(link_factor.reshape(devices, devices, capacity), (1, 0, 2))
    regime = jnp.transpose(link_regime.reshape(devices, devices, capacity), (1, 0, 2))
    target = jnp.arange(devices, dtype=jnp.int32)[None, :, None]
    global_section = (target * SEC_DEV + sections) * RIV + reaches
    channel_level = channel_segment.reshape(-1)[global_section]
    link_flow = weir_flow(channel_level, plain_level, crest, factor, regime)
    lateral = jnp.zeros((SECTIONS * RIV,), jnp.float32).at[global_section.reshape(-1)].add(-link_flow.reshape(-1)).reshape(SECTIONS, RIV)
    bank_gain = jnp.zeros((NX * NY,), jnp.float32).at[(row_index * NY + col_index).reshape(-1)].add(link_flow.reshape(-1)).reshape(NX, NY)
    wetness = wet_mask.astype(jnp.float32)
    bed_pad = jnp.pad(bed_level, 1)
    rough_pad = jnp.pad(roughness, 1)
    wet_pad = jnp.pad(wetness, 1)
    water, east, south = (water_depth, flux_east, flux_south)
    for index in range(SUBSTEPS):
        water, east, south = substep(jnp.pad(water, 1), jnp.pad(east, 1), jnp.pad(south, 1), bed_pad, rough_pad, wet_pad)
    new_depth = water + BANK_GAIN * bank_gain
    scale = 0.5 + IMPLICIT_WEIGHT * courant
    passing = jnp.where(junction == 1, pass_share, 1.0 + 0.0 * pass_share)
    carry_weight = passing * (IMPLICIT_WEIGHT * courant - 0.5) / scale
    old_weight = passing * (0.5 + (1.0 - IMPLICIT_WEIGHT) * courant) / scale
    offset = ((0.5 - (1.0 - IMPLICIT_WEIGHT) * courant) * old_discharge + LATERAL_SCALE * courant * lateral) / scale

    def advance(carry, items):
        new_prev, old_prev = carry
        weight_new, weight_old, shift, old_here = items
        value = weight_new * new_prev + weight_old * old_prev + shift
        return ((value, old_here), value)
    _, new_discharge = lax.scan(advance, (inflow, inflow), (carry_weight, old_weight, offset, old_discharge))
    return (new_depth, east, south, new_discharge)
```

```python
import functools

import jax
import jax.numpy as jnp
from jax import lax
from jax.experimental import pallas as pl
from jax.experimental.pallas import tpu as pltpu
from jax.sharding import PartitionSpec as P

GRAVITY = 9.81
SPACING = 20.0
TIME_STEP = 2.2
MIN_FLOW_DEPTH = 0.3
IMPLICIT_WEIGHT = 0.6
LATERAL_SCALE = 0.01
BANK_GAIN = 0.5
SUBSTEPS = 4

f32, bf16, i32, i16 = jnp.float32, jnp.bfloat16, jnp.int32, jnp.int16
MESH = pl.DeviceIdType.MESH

NGX, NGY = 8, 16
CX, CY = 64, 256
SEC, RIV = 32, 512
ROWS = 256
G = 64
PX, PY = CX + 8, CY + 128
STRIP = 8


def split2(x):
    hi = x.astype(bf16)
    return hi, (x - hi.astype(f32)).astype(bf16)


def one_hot(index_row, width):
    iota = lax.broadcasted_iota(i16, (width, 128), 0)
    index = jnp.broadcast_to(index_row.astype(i16), (width, 128))
    return jnp.where(iota == index, jnp.ones((), bf16), jnp.zeros((), bf16))


def gather_chunk(table, rows, cols):
    iota = lax.broadcasted_iota(i32, (64, 128), 0)
    picks = jnp.concatenate([one_hot(c, 256) for c in cols], 1)
    both = jnp.dot(table, picks, preferred_element_type=f32)
    both = both[:64] + both[64:]
    out = []
    for j, r in enumerate(rows):
        part = both[:, j * 128 : (j + 1) * 128]
        out.append(jnp.sum(jnp.where(iota == r, part, 0.0), 0, keepdims=True))
    return out


def scatter_chunk(flows, rows, cols):
    iota = lax.broadcasted_iota(i16, (64, 128), 0)
    zero = jnp.zeros((), bf16)
    picks = jnp.concatenate([one_hot(c, 256) for c in cols], 1)
    parts = []
    for flow, r in zip(flows, rows):
        hi, lo = split2(flow)
        mask = iota == jnp.broadcast_to(r.astype(i16), (64, 128))
        parts.append(
            jnp.concatenate(
                [
                    jnp.where(mask, jnp.broadcast_to(hi, (64, 128)), zero),
                    jnp.where(mask, jnp.broadcast_to(lo, (64, 128)), zero),
                ],
                0,
            )
        )
    parts = jnp.concatenate(parts, 1)
    return lax.dot_general(
        picks, parts, (((1,), (1,)), ((), ())), preferred_element_type=f32
    )


def kernel(*refs):
    hbm = refs[:19]
    depth_out, east_out, south_out, river_out = refs[19:23]
    vm = refs[23:42]
    (
        level_send,
        level_mid,
        level_turn,
        level_here,
        link_channel,
        flow_out,
        flow_mid,
        flow_turn,
        flow_here,
        halo_up,
        halo_down,
        from_north,
        from_south,
        strip_east,
        strip_west,
        from_west,
        from_east,
        old_send,
        old_before,
        map_row,
        map_col,
        fields,
        in_sem,
        gy_send,
        gy_recv,
        gx_send,
        gx_recv,
        back_gx_send,
        back_gx_recv,
        back_gy_send,
        back_gy_recv,
        halo_send,
        halo_recv,
        map_gy_send,
        map_gy_recv,
        map_gx_send,
        map_gx_recv,
    ) = refs[42:]
    (
        water, bed, rough, wet, east, south, bank_row, bank_col, link_sec, link_reach,
        crest, factor, regime, channel, old, courant, junction, share, inflow,
    ) = vm

    gx, gy = lax.axis_index("gx"), lax.axis_index("gy")

    order = [0, 1, 6, 7, 2, 3, 4, 5, 14, 13, 8, 9, 10, 11, 12, 15, 16, 17, 18]
    loads = {k: pltpu.make_async_copy(hbm[k], vm[k], in_sem.at[k]) for k in range(19)}
    for k in order:
        loads[k].start()

    chain = gx * NGY + gy
    after = lax.rem(chain + 1, NGX * NGY)
    before = lax.rem(chain + NGX * NGY - 1, NGX * NGY)
    barrier = pltpu.get_barrier_semaphore()

    def greet(where):
        pl.semaphore_signal(barrier, inc=1, device_id=where, device_id_type=MESH)

    def greet_gy(j, c):
        greet((gx, lax.rem(gy + j, NGY)))
        return c

    def greet_gx(j, c):
        greet((lax.rem(gx + j, NGX), gy))
        return c

    lax.fori_loop(1, NGY, greet_gy, 0)
    lax.fori_loop(1, NGX, greet_gx, 0)
    greet((after // NGY, lax.rem(after, NGY)))
    greet((before // NGY, lax.rem(before, NGY)))

    for k in (0, 1, 6, 7):
        loads[k].wait()
    level_table = jnp.concatenate(split2(bed[...] + water[...]), 0)

    def bank_rows(i):
        base = pl.multiple_of(i * 8, 8)
        found = []
        for j in range(G):
            there = (j & 7) * 32 + (j // 16) * 2 + ((j >> 3) & 1)
            found.append(pl.ds(base + there, 1))
        return found

    def gather_bank(i, c):
        at = bank_rows(i)
        got = gather_chunk(
            level_table, [bank_row[a, :] for a in at], [bank_col[a, :] for a in at]
        )
        level_send[pl.ds(pl.multiple_of(i * G, G), G), :] = jnp.concatenate(got, 0)
        return c

    lax.fori_loop(0, ROWS // G, gather_bank, 0)

    for k in (2, 3, 4, 5, 14):
        loads[k].wait()
    planes = (water, east, south, bed, rough, wet)
    for f, ref in enumerate(planes):
        halo_up[f] = ref[0:8, :].astype(f32)
        halo_down[f] = ref[CX - 8 : CX, :].astype(f32)
    old_send[...] = old[SEC - 1 : SEC, :]

    pl.semaphore_wait(barrier, NGX + NGY)

    def rows_of(p, n):
        return pl.ds(pl.multiple_of(p * n, n), n)

    def remote(src, dst, send, recv, where):
        return pltpu.make_async_remote_copy(
            src_ref=src, dst_ref=dst, send_sem=send, recv_sem=recv,
            device_id=where, device_id_type=MESH,
        )

    def gy_copy(src, dst, n, send, recv, p):
        return remote(
            src.at[rows_of(p, n)], dst.at[rows_of(gy, n)], send.at[p], recv.at[gy], (gx, p)
        )

    def gy_arrival(src, dst, n, send, recv, p):
        return remote(
            src.at[rows_of(p, n)], dst.at[rows_of(p, n)], send.at[p], recv.at[p], (gx, p)
        )

    def gx_copy(src, dst, n, send, recv, p):
        return remote(
            src.at[rows_of(p, n)], dst.at[rows_of(gx, n)], send.at[p], recv.at[gx], (p, gy)
        )

    def gx_arrival(src, dst, n, send, recv, p):
        return remote(
            src.at[rows_of(p, n)], dst.at[rows_of(p, n)], send.at[p], recv.at[p], (p, gy)
        )

    def gy_all(what):
        def one(j, c):
            what(lax.rem(gy + j, NGY))
            return c

        lax.fori_loop(1, NGY, one, 0)

    def gx_all(what):
        def one(j, c):
            what(lax.rem(gx + j, NGX))
            return c

        lax.fori_loop(1, NGX, one, 0)

    level_gy = (level_send, level_mid, 16, gy_send, gy_recv)
    level_gx = (level_turn, level_here, 32, gx_send, gx_recv)
    flow_gx = (flow_out, flow_mid, 32, back_gx_send, back_gx_recv)
    flow_gy = (flow_turn, flow_here, 16, back_gy_send, back_gy_recv)

    gy_all(lambda p: gy_copy(*level_gy, p).start())
    level_mid[rows_of(gy, 16), :] = level_send[rows_of(gy, 16), :]

    north, south_to = lax.rem(gx + NGX - 1, NGX), lax.rem(gx + 1, NGX)
    west, east_to = lax.rem(gy + NGY - 1, NGY), lax.rem(gy + 1, NGY)
    up_copy = remote(halo_up, from_south, halo_send.at[0], halo_recv.at[0], (north, gy))
    down_copy = remote(halo_down, from_north, halo_send.at[1], halo_recv.at[1], (south_to, gy))
    old_copy = remote(
        old_send, old_before, halo_send.at[4], halo_recv.at[4],
        (after // NGY, lax.rem(after, NGY)),
    )
    up_copy.start()
    down_copy.start()
    old_copy.start()

    for k in (13, 8, 9):
        loads[k].wait()
    channel_table = jnp.concatenate(
        split2(jnp.concatenate([channel[:, :CY], channel[:, CY:]], 0)), 0
    )

    def link_cells(i):
        base = pl.multiple_of(i * G, G)
        reach = [link_reach[pl.ds(base + j, 1), :] for j in range(G)]
        rows = [link_sec[pl.ds(base + j, 1), :] + ((q >> 8) << 5) for j, q in enumerate(reach)]
        return base, rows, [q & 255 for q in reach]

    def gather_channel(i, c):
        base, rows, cols = link_cells(i)
        link_channel[pl.ds(base, G), :] = jnp.concatenate(
            gather_chunk(channel_table, rows, cols), 0
        )
        return c

    lax.fori_loop(0, 2, gather_channel, 0)

    gy_all(lambda p: gy_arrival(*level_gy, p).wait_recv())
    for g in range(NGX):
        for k in range(4):
            level_turn[g * 32 + k * 8 : g * 32 + k * 8 + 8, :] = level_mid[
                pl.ds(g + 64 * k, 8, stride=8), :
            ]
    gx_all(lambda p: gx_copy(*level_gx, p).start())
    level_here[rows_of(gx, 32), :] = level_turn[rows_of(gx, 32), :]

    up_copy.wait_recv()
    down_copy.wait_recv()
    sub8 = lax.broadcasted_iota(i32, (8, CY), 0)
    lane = lax.broadcasted_iota(i32, (PX, 128), 1)
    pack_east = jnp.zeros((PX, 128), f32)
    pack_west = jnp.zeros((PX, 128), f32)
    for f, ref in enumerate(planes):
        beyond = jnp.where(
            sub8 < 4,
            jnp.where(gx < NGX - 1, from_south[f], 0.0),
            jnp.where(gx > 0, from_north[f], 0.0),
        )
        fields[f, 0:CX, 0:CY] = ref[...].astype(f32)
        fields[f, CX:PX, 0:CY] = beyond
        right = jnp.concatenate([ref[:, CY - 128 :].astype(f32), beyond[:, CY - 128 :]], 0)
        left = jnp.concatenate([ref[:, :128].astype(f32), beyond[:, :128]], 0)
        mine = (lane >= STRIP * f) & (lane < STRIP * f + 4)
        right = pltpu.roll(right, (STRIP * f + 4) % 128, 1)
        left = pltpu.roll(left, STRIP * f, 1) if f else left
        pack_east = jnp.where(mine, right, pack_east)
        pack_west = jnp.where(mine, left, pack_west)
    strip_east[...] = pack_east
    strip_west[...] = pack_west
    east_copy = remote(strip_east, from_west, halo_send.at[2], halo_recv.at[2], (gx, east_to))
    west_copy = remote(strip_west, from_east, halo_send.at[3], halo_recv.at[3], (gx, west))
    east_copy.start()
    west_copy.start()

    lax.fori_loop(2, 4, gather_channel, 0)

    for k in (10, 11, 12):
        loads[k].wait()
    gx_all(lambda p: gx_arrival(*level_gx, p).wait_recv())

    def flow_part(i, c):
        at = pl.ds(pl.multiple_of(i * 32, 32), 32)
        plain, chan, top, rule = level_here[at, :], link_channel[at, :], crest[at, :], regime[at, :]
        upper = jnp.maximum(chan - top, 0.0)
        lower = jnp.maximum(plain - top, 0.0)
        free = upper * jnp.sqrt(upper) - lower * jnp.sqrt(lower)
        drop = chan - plain
        drowned = drop * jnp.sqrt(jnp.abs(drop))
        flow_out[at, :] = factor[at, :] * jnp.where(
            rule == 1, free, jnp.where(rule == 2, drowned, 0.0)
        )
        return c

    lax.fori_loop(0, 8, flow_part, 0)
    gx_all(lambda p: gx_copy(*flow_gx, p).start())
    flow_mid[rows_of(gx, 32), :] = flow_out[rows_of(gx, 32), :]

    def scatter_lateral(i, acc):
        base, rows, cols = link_cells(i)
        return acc + scatter_chunk(
            [flow_out[pl.ds(base + j, 1), :] for j in range(G)], rows, cols
        )

    acc = lax.fori_loop(0, 2, scatter_lateral, jnp.zeros((CY, 128), f32))

    gx_all(lambda p: gx_arrival(*flow_gx, p).wait_recv())
    for g in range(NGY):
        for h in range(2):
            flow_turn[g * 16 + h * 8 : g * 16 + h * 8 + 8, :] = flow_mid[
                pl.ds(g * 2 + h, 8, stride=32), :
            ]
    gy_all(lambda p: gy_copy(*flow_gy, p).start())
    flow_here[rows_of(gy, 16), :] = flow_turn[rows_of(gy, 16), :]

    acc = lax.fori_loop(2, 4, scatter_lateral, acc).T
    acc = acc[:64] + acc[64:]
    lateral = -jnp.concatenate([acc[:SEC], acc[SEC:]], 1)

    for k in (15, 16, 17, 18):
        loads[k].wait()
    old_copy.wait_recv()
    cour = courant[...]
    inverse = 1.0 / (0.5 + IMPLICIT_WEIGHT * cour)
    passing = jnp.where(junction[...] == 1, share[...], 1.0)
    carry = passing * (IMPLICIT_WEIGHT * cour - 0.5) * inverse
    old_weight = passing * (0.5 + (1.0 - IMPLICIT_WEIGHT) * cour) * inverse
    here = old[...]
    sub = lax.broadcasted_iota(i32, (SEC, RIV), 0)
    previous = jnp.where(
        sub == 0,
        jnp.where(chain == 0, inflow[...], old_before[...]),
        pltpu.roll(here, 1, 0),
    )
    shift = old_weight * previous + (
        (0.5 - (1.0 - IMPLICIT_WEIGHT) * cour) * here + LATERAL_SCALE * cour * lateral
    ) * inverse
    step = 1
    while step < SEC:
        keep = sub >= step
        shift = jnp.where(keep, carry * pltpu.roll(shift, step, 0) + shift, shift)
        carry = jnp.where(keep, carry * pltpu.roll(carry, step, 0), carry)
        step *= 2
    total = jnp.concatenate([carry[SEC - 1 :], shift[SEC - 1 :]], 0)
    map_row[pl.ds(gy, 1)] = total[None]

    def map_gy(p, slot):
        return remote(
            map_row.at[gy], map_row.at[slot], map_gy_send.at[p], map_gy_recv.at[slot], (gx, p)
        )

    def map_gx(p, slot):
        return remote(
            map_col.at[gx], map_col.at[slot], map_gx_send.at[p], map_gx_recv.at[slot], (p, gy)
        )

    gy_all(lambda p: map_gy(p, gy).start())

    east_copy.wait_recv()
    west_copy.wait_recv()
    held = []
    for f in range(6):
        right = pltpu.roll(from_east[...], (128 - STRIP * f) % 128, 1) if f else from_east[...]
        left = pltpu.roll(from_west[...], (128 - STRIP * f - 4) % 128, 1)
        side = jnp.where(
            lane < 4,
            jnp.where(gy < NGY - 1, right, 0.0),
            jnp.where((lane >= 124) & (gy > 0), left, 0.0),
        )
        fields[f, :, CY:PY] = side
        held.append(fields[f])
    depth, q_east, q_south, ground, manning, wetness = held

    def of_east(a):
        return pltpu.roll(a, PY - 1, 1)

    def of_south(a):
        return pltpu.roll(a, PX - 1, 0)

    faces = []
    for move in (of_east, of_south):
        mean = 0.5 * (manning + move(manning))
        faces.append(
            (
                move,
                jnp.maximum(ground, move(ground)),
                GRAVITY * TIME_STEP * mean * mean,
                wetness * move(wetness),
            )
        )
    flux = [q_east, q_south]
    for _ in range(SUBSTEPS):
        surface = ground + depth
        for n, (move, top, rub, open_) in enumerate(faces):
            beside = move(surface)
            flow_depth = jnp.maximum(jnp.maximum(surface, beside) - top, MIN_FLOW_DEPTH)
            drive = flux[n] - (GRAVITY * TIME_STEP / SPACING) * flow_depth * (beside - surface)
            friction = 1.0 + rub * jnp.abs(flux[n]) * jnp.exp((-7.0 / 3.0) * jnp.log(flow_depth))
            flux[n] = open_ * drive / friction
        depth = depth + (TIME_STEP / SPACING) * (
            pltpu.roll(flux[0], 1, 1) - flux[0] + pltpu.roll(flux[1], 1, 0) - flux[1]
        )
    east_out[...] = flux[0][:CX, :CY]
    south_out[...] = flux[1][:CX, :CY]
    fields[0] = depth

    gy_all(lambda p: gy_arrival(*flow_gy, p).wait_recv())

    def scatter_bank(i, acc):
        at = bank_rows(i)
        base = pl.multiple_of(i * G, G)
        return acc + scatter_chunk(
            [flow_here[pl.ds(base + j, 1), :] for j in range(G)],
            [bank_row[a, :] for a in at],
            [bank_col[a, :] for a in at],
        )

    acc = lax.fori_loop(0, 1, scatter_bank, jnp.zeros((CY, 128), f32))

    gy_all(lambda p: map_gy(p, p).wait_recv())
    a_run, s_run = jnp.ones((1, RIV), f32), jnp.zeros((1, RIV), f32)
    a_in, s_in = a_run, s_run
    for j in range(NGY):
        a_in = jnp.where(j < gy + 1, a_run, a_in)
        s_in = jnp.where(j < gy + 1, s_run, s_in)
        a_j, s_j = map_row[j, 0:1, :], map_row[j, 1:2, :]
        s_run = a_j * s_run + s_j
        a_run = a_j * a_run
    map_col[pl.ds(gx, 1)] = jnp.concatenate([a_run, s_run], 0)[None]
    gx_all(lambda p: map_gx(p, gx).start())

    acc = lax.fori_loop(1, 4, scatter_bank, acc).T
    depth_out[...] = fields[0, 0:CX, 0:CY] + BANK_GAIN * (acc[:64] + acc[64:])

    gx_all(lambda p: map_gx(p, p).wait_recv())
    x = inflow[...]
    for j in range(NGX - 1):
        x = jnp.where(j < gx, map_col[j, 0:1, :] * x + map_col[j, 1:2, :], x)
    x = a_in * x + s_in
    river_out[...] = carry * x + shift

    gy_all(lambda p: gy_copy(*level_gy, p).wait_send())
    gx_all(lambda p: gx_copy(*level_gx, p).wait_send())
    gx_all(lambda p: gx_copy(*flow_gx, p).wait_send())
    gy_all(lambda p: gy_copy(*flow_gy, p).wait_send())
    gy_all(lambda p: map_gy(p, gy).wait_send())
    gx_all(lambda p: map_gx(p, gx).wait_send())
    for copy in (up_copy, down_copy, old_copy, east_copy, west_copy):
        copy.wait_send()


def on_device(*args):
    args = list(args)
    for k in range(6, 13):
        args[k] = args[k].reshape(ROWS, 128)
    args[18] = args[18].reshape(1, RIV)
    link = pltpu.VMEM((ROWS, 128), f32)
    halo_rows = pltpu.VMEM((6, 8, CY), f32)
    strip = pltpu.VMEM((PX, 128), f32)
    dma = pltpu.SemaphoreType.DMA
    scratch = [pltpu.VMEM(a.shape, a.dtype) for a in args]
    scratch += [link] * 9
    scratch += [halo_rows] * 4
    scratch += [strip] * 4
    scratch += [pltpu.VMEM((1, RIV), f32)] * 2
    scratch += [pltpu.VMEM((NGY, 2, RIV), f32), pltpu.VMEM((NGX, 2, RIV), f32)]
    scratch += [pltpu.VMEM((6, PX, PY), f32)]
    scratch += [dma((19,))]
    scratch += [dma((NGY,)), dma((NGY,)), dma((NGX,)), dma((NGX,))]
    scratch += [dma((NGX,)), dma((NGX,)), dma((NGY,)), dma((NGY,))]
    scratch += [dma((5,)), dma((5,))]
    scratch += [dma((NGY,)), dma((NGY,)), dma((NGX,)), dma((NGX,))]
    return pl.pallas_call(
        kernel,
        out_shape=(
            jax.ShapeDtypeStruct((CX, CY), f32),
            jax.ShapeDtypeStruct((CX, CY), f32),
            jax.ShapeDtypeStruct((CX, CY), f32),
            jax.ShapeDtypeStruct((SEC, RIV), f32),
        ),
        in_specs=[pl.BlockSpec(memory_space=pl.ANY)] * 19,
        out_specs=[pl.BlockSpec(memory_space=pltpu.VMEM)] * 4,
        scratch_shapes=scratch,
        compiler_params=pltpu.CompilerParams(
            collective_id=0, has_side_effects=True, vmem_limit_bytes=48 << 20
        ),
        cost_estimate=pl.CostEstimate(
            flops=8 * 10**9, bytes_accessed=2 * 10**6, transcendentals=10**6
        ),
        name="coupled_step",
    )(*args)


def solution(mesh):
    tile, flat, chain = P("gx", "gy"), P(("gx", "gy")), P(("gx", "gy"), None)
    in_specs = (tile,) * 6 + (flat,) * 7 + (chain,) * 5 + (P(),)
    out_specs = (tile, tile, tile, chain)
    return jax.shard_map(
        on_device, mesh=mesh, in_specs=in_specs, out_specs=out_specs, check_vma=False
    )
```

```python
import functools

import jax
import jax.numpy as jnp
from jax import lax
from jax.experimental import pallas as pl
from jax.experimental.pallas import tpu as pltpu
from jax.sharding import PartitionSpec as P

GRAVITY = 9.81
SPACING = 20.0
TIME_STEP = 2.2
MIN_FLOW_DEPTH = 0.3
IMPLICIT_WEIGHT = 0.6
LATERAL_SCALE = 0.01
BANK_GAIN = 0.5
SUBSTEPS = 4

f32, bf16, i32, i16 = jnp.float32, jnp.bfloat16, jnp.int32, jnp.int16
MESH = pl.DeviceIdType.MESH

NGX, NGY = 8, 16
CX, CY = 64, 256
SEC, RIV = 32, 512
ROWS = 256
G = 128
DEV = NGX * NGY
PX, PY = CX + 8, CY + 128
STRIP = 8
LANES = 128
PER = RIV // LANES


def far_first():
    steps = [
        (z, c, y, x) for z in range(4) for c in range(2) for y in range(4) for x in range(4)
    ][1:]
    far = lambda s: min(s[0], 4 - s[0]) + min(s[2], 4 - s[2]) + min(s[3], 4 - s[3]) + 0.3 * s[1]
    return sorted(steps, key=far, reverse=True)


STEPS = far_first()


def split2(x):
    hi = x.astype(bf16)
    return hi, (x - hi.astype(f32)).astype(bf16)


def one_hot(index_row, width):
    iota = lax.broadcasted_iota(i16, (width, 128), 0)
    index = jnp.broadcast_to(index_row.astype(i16), (width, 128))
    return jnp.where(iota == index, jnp.ones((), bf16), jnp.zeros((), bf16))


def gather_chunk(table, rows, cols):
    iota = lax.broadcasted_iota(i32, (64, 128), 0)
    picks = jnp.concatenate([one_hot(c, 256) for c in cols], 1)
    both = jnp.dot(table, picks, preferred_element_type=f32)
    both = both[:64] + both[64:]
    out = []
    for j, r in enumerate(rows):
        part = both[:, j * 128 : (j + 1) * 128]
        out.append(jnp.sum(jnp.where(iota == r, part, 0.0), 0, keepdims=True))
    return out


def scatter_chunk(flows, rows, cols):
    iota = lax.broadcasted_iota(i16, (64, 128), 0)
    zero = jnp.zeros((), bf16)
    picks = jnp.concatenate([one_hot(c, 256) for c in cols], 1)
    parts = []
    for flow, r in zip(flows, rows):
        hi, lo = split2(flow)
        mask = iota == jnp.broadcast_to(r.astype(i16), (64, 128))
        parts.append(
            jnp.concatenate(
                [
                    jnp.where(mask, jnp.broadcast_to(hi, (64, 128)), zero),
                    jnp.where(mask, jnp.broadcast_to(lo, (64, 128)), zero),
                ],
                0,
            )
        )
    parts = jnp.concatenate(parts, 1)
    return lax.dot_general(
        picks, parts, (((1,), (1,)), ((), ())), preferred_element_type=f32
    )


def wide(x):
    return jnp.concatenate([x[q : q + 1] for q in range(PER)], 1)


def narrow(x):
    return jnp.concatenate([x[:, q * LANES : (q + 1) * LANES] for q in range(PER)], 0)


def kernel(*refs):
    hbm = refs[:19]
    depth_out, east_out, south_out, river_out = refs[19:23]
    vm = refs[23:42]
    (
        level_send, level_here, link_channel, flow_send, flow_here,
        halo_up, halo_down, from_north, from_south,
        strip_east, strip_west, from_west, from_east, corners,
        old_send, old_before, carry_send, carry_all, shift_send, shift_all, weights,
        fields, levels, fixed, slope,
        in_sem, own_sem, send_sem, recv_sem, halo_send, halo_recv,
    ) = refs[42:]
    (
        water, bed, rough, wet, east, south, bank_row, bank_col, link_sec, link_reach,
        crest, factor, regime, channel, old, courant, junction, share, inflow,
    ) = vm

    gx, gy = lax.axis_index("gx"), lax.axis_index("gy")
    me = gx * NGY + gy
    z, core, y, x = gx // 2, lax.rem(gx, 2), gy // 4, lax.rem(gy, 4)

    order = [6, 7, 0, 1, 2, 3, 4, 5, 15, 16, 17, 14, 13, 8, 9, 10, 11, 12, 18]
    loads = {k: pltpu.make_async_copy(hbm[k], vm[k], in_sem.at[k]) for k in range(19)}
    for k in order:
        loads[k].start()

    zs = [lax.rem(z + d, 4) for d in range(4)]
    cs = [lax.rem(core + d, 2) for d in range(2)]
    ys = [lax.rem(y + d, 4) for d in range(4)]
    xs = [lax.rem(x + d, 4) for d in range(4)]
    peers = []
    for dz, dc, dy, dx in STEPS:
        px, py = zs[dz] * 2 + cs[dc], ys[dy] * 4 + xs[dx]
        peers.append((px, py, px * NGY + py))
    barrier = pltpu.get_barrier_semaphore()
    for px, py, _ in peers:
        pl.semaphore_signal(barrier, inc=1, device_id=(px, py), device_id_type=MESH)

    def remote(src, dst, send, recv, where):
        return pltpu.make_async_remote_copy(
            src_ref=src, dst_ref=dst, send_sem=send, recv_sem=recv,
            device_id=where, device_id_type=MESH,
        )

    def to_all(src, dst, n, k, same):
        for px, py, p in peers:
            remote(
                src if same else src.at[pl.ds(p * n, n)],
                dst.at[pl.ds(me * n, n)], send_sem.at[k], recv_sem.at[k], (px, py),
            ).start()
        own = pltpu.make_async_copy(
            src if same else src.at[pl.ds(me * n, n)], dst.at[pl.ds(me * n, n)], own_sem.at[k]
        )
        own.start()

        def arrived():
            part = dst.at[pl.ds(0, (DEV - 1) * n)]
            pltpu.make_async_copy(part, part, recv_sem.at[k]).wait()
            own.wait()

        def sent():
            part = dst.at[pl.ds(0, (DEV - 1) * n)]
            pltpu.make_async_copy(part, part, send_sem.at[k]).wait()

        return arrived, sent

    for k in (6, 7, 0, 1):
        loads[k].wait()
    level_table = jnp.concatenate(split2(bed[...] + water[...]), 0)

    def bank_cells(i):
        base = pl.multiple_of(i * G, G)
        at = [pl.ds(base + j, 1) for j in range(G)]
        return base, [bank_row[a, :] for a in at], [bank_col[a, :] for a in at]

    def gather_bank(i, c):
        base, rows, cols = bank_cells(i)
        level_send[pl.ds(base, G), :] = jnp.concatenate(
            gather_chunk(level_table, rows, cols), 0
        )
        return c

    lax.fori_loop(0, ROWS // G, gather_bank, 0)

    for k in (2, 3, 4, 5, 14):
        loads[k].wait()
    planes = (water, east, south, bed, rough, wet)
    lane = lax.broadcasted_iota(i32, (CX, 128), 1)
    pack_east = jnp.zeros((CX, 128), f32)
    pack_west = jnp.zeros((CX, 128), f32)
    for f, ref in enumerate(planes):
        halo_up[f] = ref[0:8, :].astype(f32)
        halo_down[f] = ref[CX - 8 : CX, :].astype(f32)
        right, left = ref[:, CY - 128 :].astype(f32), ref[:, :128].astype(f32)
        mine = (lane >= STRIP * f) & (lane < STRIP * f + 4)
        right = pltpu.roll(right, (STRIP * f + 4) % 128, 1)
        left = pltpu.roll(left, STRIP * f, 1) if f else left
        pack_east = jnp.where(mine, right, pack_east)
        pack_west = jnp.where(mine, left, pack_west)
    strip_east[...] = pack_east
    strip_west[...] = pack_west
    old_send[...] = old[SEC - 1 : SEC, :]

    pl.semaphore_wait(barrier, DEV - 1)

    level_arrived, level_sent = to_all(level_send, level_here, 2, 0, False)

    north, south_to = lax.rem(gx + NGX - 1, NGX), lax.rem(gx + 1, NGX)
    west, east_to = lax.rem(gy + NGY - 1, NGY), lax.rem(gy + 1, NGY)
    after = lax.rem(me + 1, DEV)
    top, bottom = pl.ds(0, 8), pl.ds(CX - 8, 8)
    halos = [
        (halo_up, from_south, (north, gy)),
        (halo_down, from_north, (south_to, gy)),
        (strip_east, from_west, (gx, east_to)),
        (strip_west, from_east, (gx, west)),
        (strip_east.at[top], corners.at[0], (north, east_to)),
        (strip_east.at[bottom], corners.at[1], (south_to, east_to)),
        (strip_west.at[top], corners.at[2], (north, west)),
        (strip_west.at[bottom], corners.at[3], (south_to, west)),
        (old_send, old_before, (after // NGY, lax.rem(after, NGY))),
    ]
    halos = [
        remote(src, dst, halo_send.at[k], halo_recv.at[k], where)
        for k, (src, dst, where) in enumerate(halos)
    ]
    for copy in halos:
        copy.start()

    for k in (15, 16, 17):
        loads[k].wait()
    sub = lax.broadcasted_iota(i32, (SEC, RIV), 0)
    cour = courant[...]
    inverse = 1.0 / (0.5 + IMPLICIT_WEIGHT * cour)
    passing = jnp.where(junction[...] == 1, share[...], 1.0)
    carry = passing * (IMPLICIT_WEIGHT * cour - 0.5) * inverse
    old_weight = passing * (0.5 + (1.0 - IMPLICIT_WEIGHT) * cour) * inverse
    slope[...] = LATERAL_SCALE * cour * inverse
    fixed[...] = (0.5 - (1.0 - IMPLICIT_WEIGHT) * cour) * inverse * old[...]
    levels[5] = old_weight
    for n in range(5):
        levels[n] = carry
        carry = jnp.where(sub >= (1 << n), carry * pltpu.roll(carry, 1 << n, 0), carry)
    levels[6] = carry
    carry_send[...] = narrow(carry[SEC - 1 :])

    for k in (13, 8, 9):
        loads[k].wait()
    channel_table = jnp.concatenate(
        split2(jnp.concatenate([channel[:, :CY], channel[:, CY:]], 0)), 0
    )

    def link_cells(i):
        base = pl.multiple_of(i * G, G)
        reach = [link_reach[pl.ds(base + j, 1), :] for j in range(G)]
        rows = [link_sec[pl.ds(base + j, 1), :] + ((q >> 8) << 5) for j, q in enumerate(reach)]
        return base, rows, [q & 255 for q in reach]

    def gather_channel(i, c):
        base, rows, cols = link_cells(i)
        link_channel[pl.ds(base, G), :] = jnp.concatenate(
            gather_chunk(channel_table, rows, cols), 0
        )
        return c

    lax.fori_loop(0, ROWS // G, gather_channel, 0)
    carry_arrived, carry_sent = to_all(carry_send, carry_all, PER, 1, True)

    for copy in halos:
        copy.wait_recv()
    sub8 = lax.broadcasted_iota(i32, (8, CY), 0)
    held = []
    lanes = lax.broadcasted_iota(i32, (PX, 128), 1)
    side = lax.broadcasted_iota(i32, (PX, 128), 0)
    low, high = gx < NGX - 1, gx > 0
    edge8 = lax.broadcasted_iota(i32, (8, 128), 0)
    rows_in = (side < CX) | ((side < CX + 4) & low) | ((side >= CX + 4) & high)
    strip_left = jnp.concatenate(
        [from_west[...], jnp.where(edge8 < 4, corners[0], corners[1])], 0
    )
    strip_right = jnp.concatenate(
        [from_east[...], jnp.where(edge8 < 4, corners[2], corners[3])], 0
    )
    strip_left = jnp.where(rows_in & (gy > 0), strip_left, 0.0)
    strip_right = jnp.where(rows_in & (gy < NGY - 1), strip_right, 0.0)
    for f, ref in enumerate(planes):
        beyond = jnp.where(
            sub8 < 4, jnp.where(low, from_south[f], 0.0), jnp.where(high, from_north[f], 0.0)
        )
        fields[f, 0:CX, 0:CY] = ref[...].astype(f32)
        fields[f, CX:PX, 0:CY] = beyond
        right = pltpu.roll(strip_right, (128 - STRIP * f) % 128, 1) if f else strip_right
        left = pltpu.roll(strip_left, (128 - STRIP * f - 4) % 128, 1)
        fields[f, :, CY:PY] = jnp.where(
            lanes < 4, right, jnp.where(lanes >= 124, left, 0.0)
        )
        held.append(fields[f])
    depth, q_east, q_south, ground, manning, wetness = held

    def of_east(a):
        return pltpu.roll(a, PY - 1, 1)

    def of_south(a):
        return pltpu.roll(a, PX - 1, 0)

    faces = []
    for move in (of_east, of_south):
        mean = 0.5 * (manning + move(manning))
        faces.append(
            (
                move,
                jnp.maximum(ground, move(ground)),
                GRAVITY * TIME_STEP * mean * mean,
                wetness * move(wetness),
            )
        )
    flux = [q_east, q_south]
    for _ in range(SUBSTEPS):
        surface = ground + depth
        for n, (move, top, rub, open_) in enumerate(faces):
            beside = move(surface)
            flow_depth = jnp.maximum(jnp.maximum(surface, beside) - top, MIN_FLOW_DEPTH)
            drive = flux[n] - (GRAVITY * TIME_STEP / SPACING) * flow_depth * (beside - surface)
            friction = 1.0 + rub * jnp.abs(flux[n]) * jnp.exp((-7.0 / 3.0) * jnp.log(flow_depth))
            flux[n] = open_ * drive / friction
        depth = depth + (TIME_STEP / SPACING) * (
            pltpu.roll(flux[0], 1, 1) - flux[0] + pltpu.roll(flux[1], 1, 0) - flux[1]
        )
    east_out[...] = flux[0][:CX, :CY]
    south_out[...] = flux[1][:CX, :CY]
    fields[0] = depth

    loads[18].wait()
    previous = jnp.where(
        sub == 0,
        jnp.where(me == 0, inflow[...], old_before[...]),
        pltpu.roll(old[...], 1, 0),
    )
    fixed[...] = fixed[...] + levels[5] * previous

    for k in (10, 11, 12):
        loads[k].wait()
    level_arrived()

    def flow_part(i, c):
        at = pl.ds(pl.multiple_of(i * 32, 32), 32)
        plain, chan, top, rule = level_here[at, :], link_channel[at, :], crest[at, :], regime[at, :]
        upper = jnp.maximum(chan - top, 0.0)
        lower = jnp.maximum(plain - top, 0.0)
        free = upper * jnp.sqrt(upper) - lower * jnp.sqrt(lower)
        drop = chan - plain
        drowned = drop * jnp.sqrt(jnp.abs(drop))
        flow_send[at, :] = factor[at, :] * jnp.where(
            rule == 1, free, jnp.where(rule == 2, drowned, 0.0)
        )
        return c

    lax.fori_loop(0, 8, flow_part, 0)
    flow_arrived, flow_sent = to_all(flow_send, flow_here, 2, 2, False)

    def scatter_lateral(i, acc):
        base, rows, cols = link_cells(i)
        return acc + scatter_chunk(
            [flow_send[pl.ds(base + j, 1), :] for j in range(G)], rows, cols
        )

    acc = lax.fori_loop(0, ROWS // G, scatter_lateral, jnp.zeros((CY, 128), f32)).T
    acc = acc[:64] + acc[64:]
    lateral = jnp.concatenate([acc[:SEC], acc[SEC:]], 1)

    shift = fixed[...] - slope[...] * lateral
    for n in range(5):
        shift = jnp.where(
            sub >= (1 << n), levels[n] * pltpu.roll(shift, 1 << n, 0) + shift, shift
        )
    fixed[...] = shift
    shift_send[...] = narrow(shift[SEC - 1 :])
    shift_arrived, shift_sent = to_all(shift_send, shift_all, PER, 3, True)

    carry_arrived()
    half = lax.broadcasted_iota(i32, (8, LANES), 0)
    run = jnp.ones((8, LANES), f32)
    for k in range(DEV // 2 - 1, -1, -1):
        upstream = (half // PER + 2 * k) < me
        both = jnp.where(upstream, carry_all[8 * k : 8 * k + 8, :], 1.0)
        swapped = pltpu.roll(both, 4, 0)
        weight = jnp.where(half < PER, swapped, 1.0) * run
        weights[8 * k : 8 * k + 8, :] = jnp.where(upstream, weight, 0.0)
        run = run * (both * swapped)
    start = wide(run[:PER]) * inflow[...]

    flow_arrived()

    def scatter_bank(i, acc):
        base, rows, cols = bank_cells(i)
        return acc + scatter_chunk(
            [flow_here[pl.ds(base + j, 1), :] for j in range(G)], rows, cols
        )

    acc = lax.fori_loop(0, ROWS // G, scatter_bank, jnp.zeros((CY, 128), f32)).T
    depth_out[...] = fields[0, 0:CX, 0:CY] + BANK_GAIN * (acc[:64] + acc[64:])

    shift_arrived()
    parts = [
        weights[8 * k : 8 * k + 8, :] * shift_all[8 * k : 8 * k + 8, :] for k in range(DEV // 2)
    ]
    while len(parts) > 1:
        parts = [u + v for u, v in zip(parts[::2], parts[1::2])]
    enters = start + wide(parts[0][:PER] + parts[0][PER:])
    river_out[...] = levels[6] * enters + fixed[...]

    for sent in (level_sent, carry_sent, flow_sent, shift_sent):
        sent()
    for copy in halos:
        copy.wait_send()


def on_device(*args):
    args = list(args)
    for k in range(6, 13):
        args[k] = args[k].reshape(ROWS, 128)
    args[18] = args[18].reshape(1, RIV)
    vmem = lambda *shape: pltpu.VMEM(shape, f32)
    dma = pltpu.SemaphoreType.DMA
    scratch = [pltpu.VMEM(a.shape, a.dtype) for a in args]
    scratch += [vmem(ROWS, 128)] * 5
    scratch += [vmem(6, 8, CY)] * 4
    scratch += [vmem(CX, 128)] * 4 + [vmem(4, 8, 128)]
    scratch += [vmem(1, RIV)] * 2
    scratch += [vmem(PER, LANES), vmem(DEV * PER, LANES)] * 2 + [vmem(DEV * PER, LANES)]
    scratch += [vmem(6, PX, PY), vmem(7, SEC, RIV), vmem(SEC, RIV), vmem(SEC, RIV)]
    scratch += [dma((19,)), dma((4,)), dma((4,)), dma((4,)), dma((9,)), dma((9,))]
    return pl.pallas_call(
        kernel,
        out_shape=(
            jax.ShapeDtypeStruct((CX, CY), f32),
            jax.ShapeDtypeStruct((CX, CY), f32),
            jax.ShapeDtypeStruct((CX, CY), f32),
            jax.ShapeDtypeStruct((SEC, RIV), f32),
        ),
        in_specs=[pl.BlockSpec(memory_space=pl.ANY)] * 19,
        out_specs=[pl.BlockSpec(memory_space=pltpu.VMEM)] * 4,
        scratch_shapes=scratch,
        compiler_params=pltpu.CompilerParams(
            collective_id=0, has_side_effects=True, vmem_limit_bytes=62 << 20
        ),
        cost_estimate=pl.CostEstimate(
            flops=8 * 10**9, bytes_accessed=2 * 10**6, transcendentals=10**6
        ),
        name="coupled_step",
    )(*args)


def solution(mesh):
    tile, flat, chain = P("gx", "gy"), P(("gx", "gy")), P(("gx", "gy"), None)
    in_specs = (tile,) * 6 + (flat,) * 7 + (chain,) * 5 + (P(),)
    out_specs = (tile, tile, tile, chain)
    return jax.shard_map(
        on_device, mesh=mesh, in_specs=in_specs, out_specs=out_specs, check_vma=False
    )
```

```python
import functools

import jax
import jax.numpy as jnp
from jax import lax
from jax.experimental import pallas as pl
from jax.experimental.pallas import tpu as pltpu
from jax.sharding import PartitionSpec as P

GRAVITY = 9.81
SPACING = 20.0
TIME_STEP = 2.2
MIN_FLOW_DEPTH = 0.3
IMPLICIT_WEIGHT = 0.6
LATERAL_SCALE = 0.01
BANK_GAIN = 0.5
SUBSTEPS = 4

f32, bf16, i32, i16 = jnp.float32, jnp.bfloat16, jnp.int32, jnp.int16
MESH = pl.DeviceIdType.MESH

NGX, NGY = 8, 16
CX, CY = 64, 256
SEC, RIV = 32, 512
ROWS = 256
G = 128
DEV = NGX * NGY
PX, PY = CX + 8, CY + 128
STRIP = 8
LANES = 128
PER = RIV // LANES


def far_first():
    steps = [
        (z, c, y, x) for z in range(4) for c in range(2) for y in range(4) for x in range(4)
    ][1:]
    far = lambda s: min(s[0], 4 - s[0]) + min(s[2], 4 - s[2]) + min(s[3], 4 - s[3]) + 0.3 * s[1]
    return sorted(steps, key=far, reverse=True)


STEPS = far_first()


def split2(x):
    hi = x.astype(bf16)
    return hi, (x - hi.astype(f32)).astype(bf16)


def one_hot(index_row, width):
    iota = lax.broadcasted_iota(i16, (width, 128), 0)
    index = jnp.broadcast_to(index_row.astype(i16), (width, 128))
    return jnp.where(iota == index, jnp.ones((), bf16), jnp.zeros((), bf16))


def gather_chunk(table, rows, cols):
    iota = lax.broadcasted_iota(i32, (64, 128), 0)
    picks = jnp.concatenate([one_hot(c, 256) for c in cols], 1)
    both = jnp.dot(table, picks, preferred_element_type=f32)
    both = both[:64] + both[64:]
    out = []
    for j, r in enumerate(rows):
        part = both[:, j * 128 : (j + 1) * 128]
        out.append(jnp.sum(jnp.where(iota == r, part, 0.0), 0, keepdims=True))
    return out


def scatter_chunk(flows, rows, cols):
    iota = lax.broadcasted_iota(i16, (64, 128), 0)
    zero = jnp.zeros((), bf16)
    picks = jnp.concatenate([one_hot(c, 256) for c in cols], 1)
    parts = []
    for flow, r in zip(flows, rows):
        hi, lo = split2(flow)
        mask = iota == jnp.broadcast_to(r.astype(i16), (64, 128))
        parts.append(
            jnp.concatenate(
                [
                    jnp.where(mask, jnp.broadcast_to(hi, (64, 128)), zero),
                    jnp.where(mask, jnp.broadcast_to(lo, (64, 128)), zero),
                ],
                0,
            )
        )
    parts = jnp.concatenate(parts, 1)
    return lax.dot_general(
        picks, parts, (((1,), (1,)), ((), ())), preferred_element_type=f32
    )


def wide(x):
    return jnp.concatenate([x[q : q + 1] for q in range(PER)], 1)


def narrow(x):
    return jnp.concatenate([x[:, q * LANES : (q + 1) * LANES] for q in range(PER)], 0)


def kernel(*refs):
    hbm = refs[:19]
    depth_out, east_out, south_out, river_out = refs[19:23]
    vm = refs[23:42]
    (
        level_send, level_here, link_channel, flow_send, flow_here,
        halo_up, halo_down, from_north, from_south,
        strip_east, strip_west, from_west, from_east, corners,
        old_send, old_before, carry_send, carry_all, shift_send, shift_all, weights,
        fields, levels, fixed, slope,
        in_sem, own_sem, send_sem, recv_sem, halo_send, halo_recv,
    ) = refs[42:]
    (
        water, bed, rough, wet, east, south, bank_row, bank_col, link_sec, link_reach,
        crest, factor, regime, channel, old, courant, junction, share, inflow,
    ) = vm

    gx, gy = lax.axis_index("gx"), lax.axis_index("gy")
    me = gx * NGY + gy
    z, core, y, x = gx // 2, lax.rem(gx, 2), gy // 4, lax.rem(gy, 4)

    order = [6, 7, 0, 1, 2, 3, 4, 5, 15, 16, 17, 14, 13, 8, 9, 10, 11, 12, 18]
    loads = {k: pltpu.make_async_copy(hbm[k], vm[k], in_sem.at[k]) for k in range(19)}
    for k in order:
        loads[k].start()

    zs = [lax.rem(z + d, 4) for d in range(4)]
    cs = [lax.rem(core + d, 2) for d in range(2)]
    ys = [lax.rem(y + d, 4) for d in range(4)]
    xs = [lax.rem(x + d, 4) for d in range(4)]
    peers = []
    for dz, dc, dy, dx in STEPS:
        px, py = zs[dz] * 2 + cs[dc], ys[dy] * 4 + xs[dx]
        peers.append((px, py, px * NGY + py))
    barrier = pltpu.get_barrier_semaphore()
    for px, py, _ in peers:
        pl.semaphore_signal(barrier, inc=1, device_id=(px, py), device_id_type=MESH)

    def remote(src, dst, send, recv, where):
        return pltpu.make_async_remote_copy(
            src_ref=src, dst_ref=dst, send_sem=send, recv_sem=recv,
            device_id=where, device_id_type=MESH,
        )

    def to_all(src, dst, n, k, same):
        for px, py, p in peers:
            remote(
                src if same else src.at[pl.ds(p * n, n)],
                dst.at[pl.ds(me * n, n)], send_sem.at[k], recv_sem.at[k], (px, py),
            ).start()
        own = pltpu.make_async_copy(
            src if same else src.at[pl.ds(me * n, n)], dst.at[pl.ds(me * n, n)], own_sem.at[k]
        )
        own.start()

        def arrived():
            part = dst.at[pl.ds(0, (DEV - 1) * n)]
            pltpu.make_async_copy(part, part, recv_sem.at[k]).wait()
            own.wait()

        def sent():
            part = dst.at[pl.ds(0, (DEV - 1) * n)]
            pltpu.make_async_copy(part, part, send_sem.at[k]).wait()

        return arrived, sent

    for k in (6, 7, 0, 1):
        loads[k].wait()
    level_table = jnp.concatenate(split2(bed[...] + water[...]), 0)

    def bank_cells(i):
        base = pl.multiple_of(i * G, G)
        at = [pl.ds(base + j, 1) for j in range(G)]
        return base, [bank_row[a, :] for a in at], [bank_col[a, :] for a in at]

    def gather_bank(i, c):
        base, rows, cols = bank_cells(i)
        level_send[pl.ds(base, G), :] = jnp.concatenate(
            gather_chunk(level_table, rows, cols), 0
        )
        return c

    lax.fori_loop(0, ROWS // G, gather_bank, 0)

    for k in (2, 3, 4, 5, 14):
        loads[k].wait()
    planes = (water, east, south, bed, rough, wet)
    lane = lax.broadcasted_iota(i32, (CX, 128), 1)
    pack_east = jnp.zeros((CX, 128), f32)
    pack_west = jnp.zeros((CX, 128), f32)
    for f, ref in enumerate(planes):
        halo_up[f] = ref[0:8, :].astype(f32)
        halo_down[f] = ref[CX - 8 : CX, :].astype(f32)
        right, left = ref[:, CY - 128 :].astype(f32), ref[:, :128].astype(f32)
        mine = (lane >= STRIP * f) & (lane < STRIP * f + 4)
        right = pltpu.roll(right, (STRIP * f + 4) % 128, 1)
        left = pltpu.roll(left, STRIP * f, 1) if f else left
        pack_east = jnp.where(mine, right, pack_east)
        pack_west = jnp.where(mine, left, pack_west)
    strip_east[...] = pack_east
    strip_west[...] = pack_west
    old_send[...] = old[SEC - 1 : SEC, :]

    pl.semaphore_wait(barrier, DEV - 1)

    level_arrived, level_sent = to_all(level_send, level_here, 2, 0, False)

    north, south_to = lax.rem(gx + NGX - 1, NGX), lax.rem(gx + 1, NGX)
    west, east_to = lax.rem(gy + NGY - 1, NGY), lax.rem(gy + 1, NGY)
    after = lax.rem(me + 1, DEV)
    top, bottom = pl.ds(0, 8), pl.ds(CX - 8, 8)
    halos = [
        (halo_up, from_south, (north, gy)),
        (halo_down, from_north, (south_to, gy)),
        (strip_east, from_west, (gx, east_to)),
        (strip_west, from_east, (gx, west)),
        (strip_east.at[top], corners.at[0], (north, east_to)),
        (strip_east.at[bottom], corners.at[1], (south_to, east_to)),
        (strip_west.at[top], corners.at[2], (north, west)),
        (strip_west.at[bottom], corners.at[3], (south_to, west)),
        (old_send, old_before, (after // NGY, lax.rem(after, NGY))),
    ]
    halos = [
        remote(src, dst, halo_send.at[k], halo_recv.at[k], where)
        for k, (src, dst, where) in enumerate(halos)
    ]
    for copy in halos:
        copy.start()

    for k in (15, 16, 17):
        loads[k].wait()
    sub = lax.broadcasted_iota(i32, (SEC, RIV), 0)
    cour = courant[...]
    inverse = 1.0 / (0.5 + IMPLICIT_WEIGHT * cour)
    passing = jnp.where(junction[...] == 1, share[...], 1.0)
    carry = passing * (IMPLICIT_WEIGHT * cour - 0.5) * inverse
    old_weight = passing * (0.5 + (1.0 - IMPLICIT_WEIGHT) * cour) * inverse
    slope[...] = LATERAL_SCALE * cour * inverse
    fixed[...] = (0.5 - (1.0 - IMPLICIT_WEIGHT) * cour) * inverse * old[...]
    levels[5] = old_weight
    for n in range(5):
        levels[n] = carry
        carry = jnp.where(sub >= (1 << n), carry * pltpu.roll(carry, 1 << n, 0), carry)
    levels[6] = carry
    carry_send[...] = narrow(carry[SEC - 1 :])

    for k in (13, 8, 9):
        loads[k].wait()
    channel_table = jnp.concatenate(
        split2(jnp.concatenate([channel[:, :CY], channel[:, CY:]], 0)), 0
    )

    def link_cells(i):
        base = pl.multiple_of(i * G, G)
        reach = [link_reach[pl.ds(base + j, 1), :] for j in range(G)]
        rows = [link_sec[pl.ds(base + j, 1), :] + ((q >> 8) << 5) for j, q in enumerate(reach)]
        return base, rows, [q & 255 for q in reach]

    def gather_channel(i, c):
        base, rows, cols = link_cells(i)
        link_channel[pl.ds(base, G), :] = jnp.concatenate(
            gather_chunk(channel_table, rows, cols), 0
        )
        return c

    lax.fori_loop(0, ROWS // G, gather_channel, 0)
    carry_arrived, carry_sent = to_all(carry_send, carry_all, PER, 1, True)

    for copy in halos:
        copy.wait_recv()
    sub8 = lax.broadcasted_iota(i32, (8, CY), 0)
    held = []
    lanes = lax.broadcasted_iota(i32, (PX, 128), 1)
    side = lax.broadcasted_iota(i32, (PX, 128), 0)
    low, high = gx < NGX - 1, gx > 0
    edge8 = lax.broadcasted_iota(i32, (8, 128), 0)
    rows_in = (side < CX) | ((side < CX + 4) & low) | ((side >= CX + 4) & high)
    strip_left = jnp.concatenate(
        [from_west[...], jnp.where(edge8 < 4, corners[0], corners[1])], 0
    )
    strip_right = jnp.concatenate(
        [from_east[...], jnp.where(edge8 < 4, corners[2], corners[3])], 0
    )
    strip_left = jnp.where(rows_in & (gy > 0), strip_left, 0.0)
    strip_right = jnp.where(rows_in & (gy < NGY - 1), strip_right, 0.0)
    for f, ref in enumerate(planes):
        beyond = jnp.where(
            sub8 < 4, jnp.where(low, from_south[f], 0.0), jnp.where(high, from_north[f], 0.0)
        )
        fields[f, 0:CX, 0:CY] = ref[...].astype(f32)
        fields[f, CX:PX, 0:CY] = beyond
        right = pltpu.roll(strip_right, (128 - STRIP * f) % 128, 1) if f else strip_right
        left = pltpu.roll(strip_left, (128 - STRIP * f - 4) % 128, 1)
        fields[f, :, CY:PY] = jnp.where(
            lanes < 4, right, jnp.where(lanes >= 124, left, 0.0)
        )
        held.append(fields[f])
    depth, q_east, q_south, ground, manning, wetness = held

    def of_east(a):
        return pltpu.roll(a, PY - 1, 1)

    def of_south(a):
        return pltpu.roll(a, PX - 1, 0)

    faces = []
    for move in (of_east, of_south):
        mean = 0.5 * (manning + move(manning))
        faces.append(
            (
                move,
                jnp.maximum(ground, move(ground)),
                GRAVITY * TIME_STEP * mean * mean,
                wetness * move(wetness),
            )
        )
    flux = [q_east, q_south]
    for _ in range(SUBSTEPS):
        surface = ground + depth
        for n, (move, top, rub, open_) in enumerate(faces):
            beside = move(surface)
            flow_depth = jnp.maximum(jnp.maximum(surface, beside) - top, MIN_FLOW_DEPTH)
            drive = flux[n] - (GRAVITY * TIME_STEP / SPACING) * flow_depth * (beside - surface)
            friction = 1.0 + rub * jnp.abs(flux[n]) * jnp.exp((-7.0 / 3.0) * jnp.log(flow_depth))
            flux[n] = open_ * drive / friction
        depth = depth + (TIME_STEP / SPACING) * (
            pltpu.roll(flux[0], 1, 1) - flux[0] + pltpu.roll(flux[1], 1, 0) - flux[1]
        )
    east_out[...] = flux[0][:CX, :CY]
    south_out[...] = flux[1][:CX, :CY]
    fields[0] = depth

    loads[18].wait()
    previous = jnp.where(
        sub == 0,
        jnp.where(me == 0, inflow[...], old_before[...]),
        pltpu.roll(old[...], 1, 0),
    )
    fixed[...] = fixed[...] + levels[5] * previous

    for k in (10, 11, 12):
        loads[k].wait()
    level_arrived()

    def flow_part(i, c):
        at = pl.ds(pl.multiple_of(i * 32, 32), 32)
        plain, chan, top, rule = level_here[at, :], link_channel[at, :], crest[at, :], regime[at, :]
        upper = jnp.maximum(chan - top, 0.0)
        lower = jnp.maximum(plain - top, 0.0)
        free = upper * jnp.sqrt(upper) - lower * jnp.sqrt(lower)
        drop = chan - plain
        drowned = drop * jnp.sqrt(jnp.abs(drop))
        flow_send[at, :] = factor[at, :] * jnp.where(
            rule == 1, free, jnp.where(rule == 2, drowned, 0.0)
        )
        return c

    lax.fori_loop(0, 8, flow_part, 0)
    flow_arrived, flow_sent = to_all(flow_send, flow_here, 2, 2, False)

    def scatter_lateral(i, acc):
        base, rows, cols = link_cells(i)
        return acc + scatter_chunk(
            [flow_send[pl.ds(base + j, 1), :] for j in range(G)], rows, cols
        )

    acc = lax.fori_loop(0, ROWS // G, scatter_lateral, jnp.zeros((CY, 128), f32)).T
    acc = acc[:64] + acc[64:]
    lateral = jnp.concatenate([acc[:SEC], acc[SEC:]], 1)

    shift = fixed[...] - slope[...] * lateral
    for n in range(5):
        shift = jnp.where(
            sub >= (1 << n), levels[n] * pltpu.roll(shift, 1 << n, 0) + shift, shift
        )
    fixed[...] = shift
    shift_send[...] = narrow(shift[SEC - 1 :])
    shift_arrived, shift_sent = to_all(shift_send, shift_all, PER, 3, True)

    carry_arrived()
    half = lax.broadcasted_iota(i32, (8, LANES), 0)
    run = jnp.ones((8, LANES), f32)
    for k in range(DEV // 2 - 1, -1, -1):
        upstream = (half // PER + 2 * k) < me
        both = jnp.where(upstream, carry_all[8 * k : 8 * k + 8, :], 1.0)
        swapped = pltpu.roll(both, 4, 0)
        weight = jnp.where(half < PER, swapped, 1.0) * run
        weights[8 * k : 8 * k + 8, :] = jnp.where(upstream, weight, 0.0)
        run = run * (both * swapped)
    start = wide(run[:PER]) * inflow[...]

    flow_arrived()

    def scatter_bank(i, acc):
        base, rows, cols = bank_cells(i)
        return acc + scatter_chunk(
            [flow_here[pl.ds(base + j, 1), :] for j in range(G)], rows, cols
        )

    acc = lax.fori_loop(0, ROWS // G, scatter_bank, jnp.zeros((CY, 128), f32)).T
    depth_out[...] = fields[0, 0:CX, 0:CY] + BANK_GAIN * (acc[:64] + acc[64:])

    shift_arrived()
    parts = [
        weights[8 * k : 8 * k + 8, :] * shift_all[8 * k : 8 * k + 8, :] for k in range(DEV // 2)
    ]
    while len(parts) > 1:
        parts = [u + v for u, v in zip(parts[::2], parts[1::2])]
    enters = start + wide(parts[0][:PER] + parts[0][PER:])
    river_out[...] = levels[6] * enters + fixed[...]

    for sent in (level_sent, carry_sent, flow_sent, shift_sent):
        sent()
    for copy in halos:
        copy.wait_send()


def write_out(*refs):
    copies = [pltpu.make_async_copy(refs[k], refs[4 + k], refs[8].at[k]) for k in range(4)]
    for copy in copies:
        copy.start()
    for copy in copies:
        copy.wait()


def on_device(*args):
    args = list(args)
    for k in range(6, 13):
        args[k] = args[k].reshape(ROWS, 128)
    args[18] = args[18].reshape(1, RIV)
    vmem = lambda *shape: pltpu.VMEM(shape, f32)
    dma = pltpu.SemaphoreType.DMA
    scratch = [pltpu.VMEM(a.shape, a.dtype) for a in args]
    scratch += [vmem(ROWS, 128)] * 5
    scratch += [vmem(6, 8, CY)] * 4
    scratch += [vmem(CX, 128)] * 4 + [vmem(4, 8, 128)]
    scratch += [vmem(1, RIV)] * 2
    scratch += [vmem(PER, LANES), vmem(DEV * PER, LANES)] * 2 + [vmem(DEV * PER, LANES)]
    scratch += [vmem(6, PX, PY), vmem(7, SEC, RIV), vmem(SEC, RIV), vmem(SEC, RIV)]
    scratch += [dma((19,)), dma((4,)), dma((4,)), dma((4,)), dma((9,)), dma((9,))]
    results = pl.pallas_call(
        kernel,
        out_shape=(vmem(CX, CY), vmem(CX, CY), vmem(CX, CY), vmem(SEC, RIV)),
        in_specs=[pl.BlockSpec(memory_space=pl.ANY)] * 19,
        out_specs=[pl.BlockSpec(memory_space=pltpu.VMEM)] * 4,
        scratch_shapes=scratch,
        compiler_params=pltpu.CompilerParams(
            collective_id=0, has_side_effects=True, vmem_limit_bytes=62 << 20
        ),
        cost_estimate=pl.CostEstimate(
            flops=8 * 10**9, bytes_accessed=2 * 10**6, transcendentals=10**6
        ),
        name="coupled_step",
    )(*args)
    return pl.pallas_call(
        write_out,
        out_shape=[jax.ShapeDtypeStruct(r.shape, f32) for r in results],
        in_specs=[pl.BlockSpec(memory_space=pltpu.VMEM)] * 4,
        out_specs=[pl.BlockSpec(memory_space=pl.ANY)] * 4,
        scratch_shapes=[dma((4,))],
        name="write_out",
    )(*[pltpu.with_memory_space_constraint(r, pltpu.VMEM) for r in results])


def solution(mesh):
    tile, flat, chain = P("gx", "gy"), P(("gx", "gy")), P(("gx", "gy"), None)
    in_specs = (tile,) * 6 + (flat,) * 7 + (chain,) * 5 + (P(),)
    out_specs = (tile, tile, tile, chain)
    return jax.shard_map(
        on_device, mesh=mesh, in_specs=in_specs, out_specs=out_specs, check_vma=False
    )
```

```python
import functools

import jax
import jax.numpy as jnp
from jax import lax
from jax.experimental import pallas as pl
from jax.experimental.pallas import tpu as pltpu
from jax.sharding import PartitionSpec as P

GRAVITY = 9.81
SPACING = 20.0
TIME_STEP = 2.2
MIN_FLOW_DEPTH = 0.3
IMPLICIT_WEIGHT = 0.6
LATERAL_SCALE = 0.01
BANK_GAIN = 0.5
SUBSTEPS = 4

f32, bf16, i32, i16 = jnp.float32, jnp.bfloat16, jnp.int32, jnp.int16
MESH = pl.DeviceIdType.MESH

NGX, NGY = 8, 16
CX, CY = 64, 256
SEC, RIV = 32, 512
ROWS = 256
G = 128
DEV = NGX * NGY
PX, PY = CX + 8, CY + 128
STRIP = 8
LANES = 128
PER = RIV // LANES


def far_first():
    steps = [
        (z, c, y, x) for z in range(4) for c in range(2) for y in range(4) for x in range(4)
    ][1:]
    far = lambda s: min(s[0], 4 - s[0]) + min(s[2], 4 - s[2]) + min(s[3], 4 - s[3]) + 0.3 * s[1]
    return sorted(steps, key=far, reverse=True)


STEPS = far_first()


def split2(x):
    hi = x.astype(bf16)
    return hi, (x - hi.astype(f32)).astype(bf16)


def one_hot(index_row, width):
    iota = lax.broadcasted_iota(i16, (width, 128), 0)
    index = jnp.broadcast_to(index_row.astype(i16), (width, 128))
    return jnp.where(iota == index, jnp.ones((), bf16), jnp.zeros((), bf16))


def gather_chunk(table, rows, cols):
    iota = lax.broadcasted_iota(i32, (64, 128), 0)
    picks = jnp.concatenate([one_hot(c, 256) for c in cols], 1)
    both = jnp.dot(table, picks, preferred_element_type=f32)
    both = both[:64] + both[64:]
    out = []
    for j, r in enumerate(rows):
        part = both[:, j * 128 : (j + 1) * 128]
        out.append(jnp.sum(jnp.where(iota == r, part, 0.0), 0, keepdims=True))
    return out


def scatter_chunk(flows, rows, cols):
    iota = lax.broadcasted_iota(i16, (64, 128), 0)
    zero = jnp.zeros((), bf16)
    picks = jnp.concatenate([one_hot(c, 256) for c in cols], 1)
    parts = []
    for flow, r in zip(flows, rows):
        hi, lo = split2(flow)
        mask = iota == jnp.broadcast_to(r.astype(i16), (64, 128))
        parts.append(
            jnp.concatenate(
                [
                    jnp.where(mask, jnp.broadcast_to(hi, (64, 128)), zero),
                    jnp.where(mask, jnp.broadcast_to(lo, (64, 128)), zero),
                ],
                0,
            )
        )
    parts = jnp.concatenate(parts, 1)
    return lax.dot_general(
        picks, parts, (((1,), (1,)), ((), ())), preferred_element_type=f32
    )


def wide(x):
    return jnp.concatenate([x[q : q + 1] for q in range(PER)], 1)


def narrow(x):
    return jnp.concatenate([x[:, q * LANES : (q + 1) * LANES] for q in range(PER)], 0)


def kernel(*refs):
    hbm = refs[:19]
    depth_out, east_out, south_out, river_out = refs[19:23]
    vm = refs[23:42]
    (
        level_send, level_here, link_channel, flow_send, flow_here,
        halo_up, halo_down, from_north, from_south,
        strip_east, strip_west, from_west, from_east, corners,
        old_send, old_before, carry_send, carry_all, shift_send, shift_all, weights,
        fields, levels, fixed, slope,
        in_sem, own_sem, send_sem, recv_sem, halo_send, halo_recv,
    ) = refs[42:]
    (
        water, bed, rough, wet, east, south, bank_row, bank_col, link_sec, link_reach,
        crest, factor, regime, channel, old, courant, junction, share, inflow,
    ) = vm

    gx, gy = lax.axis_index("gx"), lax.axis_index("gy")
    me = gx * NGY + gy
    z, core, y, x = gx // 2, lax.rem(gx, 2), gy // 4, lax.rem(gy, 4)

    order = [6, 7, 0, 1, 2, 3, 4, 5, 15, 16, 17, 14, 13, 8, 9, 10, 11, 12, 18]
    loads = {k: pltpu.make_async_copy(hbm[k], vm[k], in_sem.at[k]) for k in range(19)}

    for k in order[:4]:
        loads[k].start()

    zs = [lax.rem(z + d, 4) for d in range(4)]
    cs = [lax.rem(core + d, 2) for d in range(2)]
    ys = [lax.rem(y + d, 4) for d in range(4)]
    xs = [lax.rem(x + d, 4) for d in range(4)]
    peers = []
    for dz, dc, dy, dx in STEPS:
        px, py = zs[dz] * 2 + cs[dc], ys[dy] * 4 + xs[dx]
        peers.append((px, py, px * NGY + py))
    barrier = pltpu.get_barrier_semaphore()
    for px, py, _ in peers:
        pl.semaphore_signal(barrier, inc=1, device_id=(px, py), device_id_type=MESH)
    for k in order[4:]:
        loads[k].start()

    def remote(src, dst, send, recv, where):
        return pltpu.make_async_remote_copy(
            src_ref=src, dst_ref=dst, send_sem=send, recv_sem=recv,
            device_id=where, device_id_type=MESH,
        )

    def to_all(src, dst, n, k, same):
        for px, py, p in peers:
            remote(
                src if same else src.at[pl.ds(p * n, n)],
                dst.at[pl.ds(me * n, n)], send_sem.at[k], recv_sem.at[k], (px, py),
            ).start()
        own = pltpu.make_async_copy(
            src if same else src.at[pl.ds(me * n, n)], dst.at[pl.ds(me * n, n)], own_sem.at[k]
        )
        own.start()

        def arrived():
            part = dst.at[pl.ds(0, (DEV - 1) * n)]
            pltpu.make_async_copy(part, part, recv_sem.at[k]).wait()
            own.wait()

        def sent():
            part = dst.at[pl.ds(0, (DEV - 1) * n)]
            pltpu.make_async_copy(part, part, send_sem.at[k]).wait()

        return arrived, sent

    for k in (6, 7, 0, 1):
        loads[k].wait()
    level_table = jnp.concatenate(split2(bed[...] + water[...]), 0)

    def bank_cells(i):
        base = pl.multiple_of(i * G, G)
        at = [pl.ds(base + j, 1) for j in range(G)]
        return base, [bank_row[a, :] for a in at], [bank_col[a, :] for a in at]

    def gather_bank(i, c):
        base, rows, cols = bank_cells(i)
        level_send[pl.ds(base, G), :] = jnp.concatenate(
            gather_chunk(level_table, rows, cols), 0
        )
        return c

    lax.fori_loop(0, ROWS // G, gather_bank, 0)

    for k in (2, 3, 4, 5, 14):
        loads[k].wait()
    planes = (water, east, south, bed, rough, wet)
    lane = lax.broadcasted_iota(i32, (CX, 128), 1)
    pack_east = jnp.zeros((CX, 128), f32)
    pack_west = jnp.zeros((CX, 128), f32)
    for f, ref in enumerate(planes):
        halo_up[f] = ref[0:8, :].astype(f32)
        halo_down[f] = ref[CX - 8 : CX, :].astype(f32)
        right, left = ref[:, CY - 128 :].astype(f32), ref[:, :128].astype(f32)
        mine = (lane >= STRIP * f) & (lane < STRIP * f + 4)
        right = pltpu.roll(right, (STRIP * f + 4) % 128, 1)
        left = pltpu.roll(left, STRIP * f, 1) if f else left
        pack_east = jnp.where(mine, right, pack_east)
        pack_west = jnp.where(mine, left, pack_west)
    strip_east[...] = pack_east
    strip_west[...] = pack_west
    old_send[...] = old[SEC - 1 : SEC, :]

    pl.semaphore_wait(barrier, DEV - 1)

    level_arrived, level_sent = to_all(level_send, level_here, 2, 0, False)

    north, south_to = lax.rem(gx + NGX - 1, NGX), lax.rem(gx + 1, NGX)
    west, east_to = lax.rem(gy + NGY - 1, NGY), lax.rem(gy + 1, NGY)
    after = lax.rem(me + 1, DEV)
    top, bottom = pl.ds(0, 8), pl.ds(CX - 8, 8)
    halos = [
        (halo_up, from_south, (north, gy)),
        (halo_down, from_north, (south_to, gy)),
        (strip_east, from_west, (gx, east_to)),
        (strip_west, from_east, (gx, west)),
        (strip_east.at[top], corners.at[0], (north, east_to)),
        (strip_east.at[bottom], corners.at[1], (south_to, east_to)),
        (strip_west.at[top], corners.at[2], (north, west)),
        (strip_west.at[bottom], corners.at[3], (south_to, west)),
        (old_send, old_before, (after // NGY, lax.rem(after, NGY))),
    ]
    halos = [
        remote(src, dst, halo_send.at[k], halo_recv.at[k], where)
        for k, (src, dst, where) in enumerate(halos)
    ]
    for copy in halos:
        copy.start()

    for k in (15, 16, 17):
        loads[k].wait()
    sub = lax.broadcasted_iota(i32, (SEC, RIV), 0)
    cour = courant[...]
    inverse = 1.0 / (0.5 + IMPLICIT_WEIGHT * cour)
    passing = jnp.where(junction[...] == 1, share[...], 1.0)
    carry = passing * (IMPLICIT_WEIGHT * cour - 0.5) * inverse
    old_weight = passing * (0.5 + (1.0 - IMPLICIT_WEIGHT) * cour) * inverse
    slope[...] = LATERAL_SCALE * cour * inverse
    fixed[...] = (0.5 - (1.0 - IMPLICIT_WEIGHT) * cour) * inverse * old[...]
    levels[5] = old_weight
    for n in range(5):
        levels[n] = carry
        carry = jnp.where(sub >= (1 << n), carry * pltpu.roll(carry, 1 << n, 0), carry)
    levels[6] = carry
    carry_send[...] = narrow(carry[SEC - 1 :])

    for k in (13, 8, 9):
        loads[k].wait()
    channel_table = jnp.concatenate(
        split2(jnp.concatenate([channel[:, :CY], channel[:, CY:]], 0)), 0
    )

    def link_cells(i):
        base = pl.multiple_of(i * G, G)
        reach = [link_reach[pl.ds(base + j, 1), :] for j in range(G)]
        rows = [link_sec[pl.ds(base + j, 1), :] + ((q >> 8) << 5) for j, q in enumerate(reach)]
        return base, rows, [q & 255 for q in reach]

    def gather_channel(i, c):
        base, rows, cols = link_cells(i)
        link_channel[pl.ds(base, G), :] = jnp.concatenate(
            gather_chunk(channel_table, rows, cols), 0
        )
        return c

    lax.fori_loop(0, ROWS // G, gather_channel, 0)
    carry_arrived, carry_sent = to_all(carry_send, carry_all, PER, 1, True)

    halos[8].wait_recv()
    loads[18].wait()
    previous = jnp.where(
        sub == 0,
        jnp.where(me == 0, inflow[...], old_before[...]),
        pltpu.roll(old[...], 1, 0),
    )
    fixed[...] = fixed[...] + levels[5] * previous

    for k in (10, 11, 12):
        loads[k].wait()
    level_arrived()

    def flow_part(i, c):
        at = pl.ds(pl.multiple_of(i * 32, 32), 32)
        plain, chan, top, rule = level_here[at, :], link_channel[at, :], crest[at, :], regime[at, :]
        upper = jnp.maximum(chan - top, 0.0)
        lower = jnp.maximum(plain - top, 0.0)
        free = upper * jnp.sqrt(upper) - lower * jnp.sqrt(lower)
        drop = chan - plain
        drowned = drop * jnp.sqrt(jnp.abs(drop))
        flow_send[at, :] = factor[at, :] * jnp.where(
            rule == 1, free, jnp.where(rule == 2, drowned, 0.0)
        )
        return c

    lax.fori_loop(0, 8, flow_part, 0)
    flow_arrived, flow_sent = to_all(flow_send, flow_here, 2, 2, False)

    def scatter_lateral(i, acc):
        base, rows, cols = link_cells(i)
        return acc + scatter_chunk(
            [flow_send[pl.ds(base + j, 1), :] for j in range(G)], rows, cols
        )

    acc = lax.fori_loop(0, ROWS // G, scatter_lateral, jnp.zeros((CY, 128), f32)).T
    acc = acc[:64] + acc[64:]
    lateral = jnp.concatenate([acc[:SEC], acc[SEC:]], 1)

    shift = fixed[...] - slope[...] * lateral
    for n in range(5):
        shift = jnp.where(
            sub >= (1 << n), levels[n] * pltpu.roll(shift, 1 << n, 0) + shift, shift
        )
    fixed[...] = shift
    shift_send[...] = narrow(shift[SEC - 1 :])
    shift_arrived, shift_sent = to_all(shift_send, shift_all, PER, 3, True)

    for copy in halos[:8]:
        copy.wait_recv()
    sub8 = lax.broadcasted_iota(i32, (8, CY), 0)
    held = []
    lanes = lax.broadcasted_iota(i32, (PX, 128), 1)
    side = lax.broadcasted_iota(i32, (PX, 128), 0)
    low, high = gx < NGX - 1, gx > 0
    edge8 = lax.broadcasted_iota(i32, (8, 128), 0)
    rows_in = (side < CX) | ((side < CX + 4) & low) | ((side >= CX + 4) & high)
    strip_left = jnp.concatenate(
        [from_west[...], jnp.where(edge8 < 4, corners[0], corners[1])], 0
    )
    strip_right = jnp.concatenate(
        [from_east[...], jnp.where(edge8 < 4, corners[2], corners[3])], 0
    )
    strip_left = jnp.where(rows_in & (gy > 0), strip_left, 0.0)
    strip_right = jnp.where(rows_in & (gy < NGY - 1), strip_right, 0.0)
    for f, ref in enumerate(planes):
        beyond = jnp.where(
            sub8 < 4, jnp.where(low, from_south[f], 0.0), jnp.where(high, from_north[f], 0.0)
        )
        fields[f, 0:CX, 0:CY] = ref[...].astype(f32)
        fields[f, CX:PX, 0:CY] = beyond
        right = pltpu.roll(strip_right, (128 - STRIP * f) % 128, 1) if f else strip_right
        left = pltpu.roll(strip_left, (128 - STRIP * f - 4) % 128, 1)
        fields[f, :, CY:PY] = jnp.where(
            lanes < 4, right, jnp.where(lanes >= 124, left, 0.0)
        )
        held.append(fields[f])
    depth, q_east, q_south, ground, manning, wetness = held

    def of_east(a):
        return pltpu.roll(a, PY - 1, 1)

    def of_south(a):
        return pltpu.roll(a, PX - 1, 0)

    faces = []
    for move in (of_east, of_south):
        mean = 0.5 * (manning + move(manning))
        faces.append(
            (
                move,
                jnp.maximum(ground, move(ground)),
                GRAVITY * TIME_STEP * mean * mean,
                wetness * move(wetness),
            )
        )
    flux = [q_east, q_south]
    for _ in range(SUBSTEPS):
        surface = ground + depth
        for n, (move, top, rub, open_) in enumerate(faces):
            beside = move(surface)
            flow_depth = jnp.maximum(jnp.maximum(surface, beside) - top, MIN_FLOW_DEPTH)
            drive = flux[n] - (GRAVITY * TIME_STEP / SPACING) * flow_depth * (beside - surface)
            friction = 1.0 + rub * jnp.abs(flux[n]) * jnp.exp((-7.0 / 3.0) * jnp.log(flow_depth))
            flux[n] = open_ * drive / friction
        depth = depth + (TIME_STEP / SPACING) * (
            pltpu.roll(flux[0], 1, 1) - flux[0] + pltpu.roll(flux[1], 1, 0) - flux[1]
        )
    east_out[...] = flux[0][:CX, :CY]
    south_out[...] = flux[1][:CX, :CY]
    fields[0] = depth

    carry_arrived()
    half = lax.broadcasted_iota(i32, (8, LANES), 0)
    run = jnp.ones((8, LANES), f32)
    for k in range(DEV // 2 - 1, -1, -1):
        upstream = (half // PER + 2 * k) < me
        both = jnp.where(upstream, carry_all[8 * k : 8 * k + 8, :], 1.0)
        swapped = pltpu.roll(both, 4, 0)
        weight = jnp.where(half < PER, swapped, 1.0) * run
        weights[8 * k : 8 * k + 8, :] = jnp.where(upstream, weight, 0.0)
        run = run * (both * swapped)
    start = wide(run[:PER]) * inflow[...]

    flow_arrived()

    def scatter_bank(i, acc):
        base, rows, cols = bank_cells(i)
        return acc + scatter_chunk(
            [flow_here[pl.ds(base + j, 1), :] for j in range(G)], rows, cols
        )

    acc = lax.fori_loop(0, ROWS // G, scatter_bank, jnp.zeros((CY, 128), f32)).T
    depth_out[...] = fields[0, 0:CX, 0:CY] + BANK_GAIN * (acc[:64] + acc[64:])

    shift_arrived()
    parts = [
        weights[8 * k : 8 * k + 8, :] * shift_all[8 * k : 8 * k + 8, :] for k in range(DEV // 2)
    ]
    while len(parts) > 1:
        parts = [u + v for u, v in zip(parts[::2], parts[1::2])]
    enters = start + wide(parts[0][:PER] + parts[0][PER:])
    river_out[...] = levels[6] * enters + fixed[...]

    for sent in (level_sent, carry_sent, flow_sent, shift_sent):
        sent()
    for copy in halos:
        copy.wait_send()


def write_out(*refs):
    copies = [pltpu.make_async_copy(refs[k], refs[4 + k], refs[8].at[k]) for k in range(4)]
    for copy in copies:
        copy.start()
    for copy in copies:
        copy.wait()


def on_device(*args):
    args = list(args)
    for k in range(6, 13):
        args[k] = args[k].reshape(ROWS, 128)
    args[18] = args[18].reshape(1, RIV)
    vmem = lambda *shape: pltpu.VMEM(shape, f32)
    dma = pltpu.SemaphoreType.DMA
    scratch = [pltpu.VMEM(a.shape, a.dtype) for a in args]
    scratch += [vmem(ROWS, 128)] * 5
    scratch += [vmem(6, 8, CY)] * 4
    scratch += [vmem(CX, 128)] * 4 + [vmem(4, 8, 128)]
    scratch += [vmem(1, RIV)] * 2
    scratch += [vmem(PER, LANES), vmem(DEV * PER, LANES)] * 2 + [vmem(DEV * PER, LANES)]
    scratch += [vmem(6, PX, PY), vmem(7, SEC, RIV), vmem(SEC, RIV), vmem(SEC, RIV)]
    scratch += [dma((19,)), dma((4,)), dma((4,)), dma((4,)), dma((9,)), dma((9,))]
    results = pl.pallas_call(
        kernel,
        out_shape=(vmem(CX, CY), vmem(CX, CY), vmem(CX, CY), vmem(SEC, RIV)),
        in_specs=[pl.BlockSpec(memory_space=pl.ANY)] * 19,
        out_specs=[pl.BlockSpec(memory_space=pltpu.VMEM)] * 4,
        scratch_shapes=scratch,
        compiler_params=pltpu.CompilerParams(
            collective_id=0, has_side_effects=True, vmem_limit_bytes=62 << 20
        ),
        cost_estimate=pl.CostEstimate(
            flops=8 * 10**9, bytes_accessed=2 * 10**6, transcendentals=10**6
        ),
        name="coupled_step",
    )(*args)
    return pl.pallas_call(
        write_out,
        out_shape=[jax.ShapeDtypeStruct(r.shape, f32) for r in results],
        in_specs=[pl.BlockSpec(memory_space=pltpu.VMEM)] * 4,
        out_specs=[pl.BlockSpec(memory_space=pl.ANY)] * 4,
        scratch_shapes=[dma((4,))],
        name="write_out",
    )(*[pltpu.with_memory_space_constraint(r, pltpu.VMEM) for r in results])


def solution(mesh):
    tile, flat, chain = P("gx", "gy"), P(("gx", "gy")), P(("gx", "gy"), None)
    in_specs = (tile,) * 6 + (flat,) * 7 + (chain,) * 5 + (P(),)
    out_specs = (tile, tile, tile, chain)
    return jax.shard_map(
        on_device, mesh=mesh, in_specs=in_specs, out_specs=out_specs, check_vma=False
    )
```

```python
import functools

import jax
import jax.numpy as jnp
from jax import lax
from jax.experimental import pallas as pl
from jax.experimental.pallas import tpu as pltpu
from jax.sharding import PartitionSpec as P

GRAVITY = 9.81
SPACING = 20.0
TIME_STEP = 2.2
MIN_FLOW_DEPTH = 0.3
IMPLICIT_WEIGHT = 0.6
LATERAL_SCALE = 0.01
BANK_GAIN = 0.5
SUBSTEPS = 4

f32, bf16, i32, i16 = jnp.float32, jnp.bfloat16, jnp.int32, jnp.int16
MESH = pl.DeviceIdType.MESH

NGX, NGY = 8, 16
CX, CY = 64, 256
SEC, RIV = 32, 512
ROWS = 256
G = 128
DEV = NGX * NGY
PX, PY = CX + 8, CY + 128
STRIP = 8
LANES = 128
PER = RIV // LANES


def far_first():
    steps = [
        (z, c, y, x) for z in range(4) for c in range(2) for y in range(4) for x in range(4)
    ][1:]
    far = lambda s: min(s[0], 4 - s[0]) + min(s[2], 4 - s[2]) + min(s[3], 4 - s[3]) + 0.3 * s[1]
    return sorted(steps, key=far, reverse=True)


STEPS = far_first()


def split2(x):
    hi = x.astype(bf16)
    return hi, (x - hi.astype(f32)).astype(bf16)


def one_hot(index_row, width):
    iota = lax.broadcasted_iota(i16, (width, 128), 0)
    index = jnp.broadcast_to(index_row.astype(i16), (width, 128))
    return jnp.where(iota == index, jnp.ones((), bf16), jnp.zeros((), bf16))


def gather_chunk(table, rows, picks):
    iota = lax.broadcasted_iota(i32, (64, 128), 0)
    picks = jnp.concatenate(picks, 1)
    both = jnp.dot(table, picks, preferred_element_type=f32)
    both = both[:64] + both[64:]
    out = []
    for j, r in enumerate(rows):
        part = both[:, j * 128 : (j + 1) * 128]
        out.append(jnp.sum(jnp.where(iota == r, part, 0.0), 0, keepdims=True))
    return out


def row_parts(flows, rows):
    iota = lax.broadcasted_iota(i16, (64, 128), 0)
    zero = jnp.zeros((), bf16)
    parts = []
    for flow, r in zip(flows, rows):
        mask = iota == jnp.broadcast_to(r.astype(i16), (64, 128))
        parts.append(
            jnp.concatenate(
                [jnp.where(mask, jnp.broadcast_to(p, (64, 128)), zero) for p in split2(flow)], 0
            )
        )
    return jnp.concatenate(parts, 1)


def scatter_chunk(flows, rows, cols):
    picks = jnp.concatenate([one_hot(c, 256) for c in cols], 1)
    return lax.dot_general(
        picks, row_parts(flows, rows), (((1,), (1,)), ((), ())), preferred_element_type=f32
    )


def wide(x):
    return jnp.concatenate([x[q : q + 1] for q in range(PER)], 1)


def narrow(x):
    return jnp.concatenate([x[:, q * LANES : (q + 1) * LANES] for q in range(PER)], 0)


def kernel(*refs):
    hbm = refs[:19]
    depth_out, east_out, south_out, river_out = refs[19:23]
    vm = refs[23:42]
    (
        level_send, level_here, link_channel, flow_send, flow_here,
        halo_up, halo_down, from_north, from_south,
        strip_east, strip_west, from_west, from_east, corners,
        old_send, old_before, carry_send, carry_all, shift_send, shift_all, weights,
        fields, levels, fixed, slope, link_picks,
        in_sem, own_sem, send_sem, recv_sem, halo_send, halo_recv,
    ) = refs[42:]
    (
        water, bed, rough, wet, east, south, bank_row, bank_col, link_sec, link_reach,
        crest, factor, regime, channel, old, courant, junction, share, inflow,
    ) = vm

    gx, gy = lax.axis_index("gx"), lax.axis_index("gy")
    me = gx * NGY + gy
    z, core, y, x = gx // 2, lax.rem(gx, 2), gy // 4, lax.rem(gy, 4)

    order = [6, 7, 0, 1, 2, 3, 4, 5, 15, 16, 17, 14, 13, 8, 9, 10, 11, 12, 18]
    loads = {k: pltpu.make_async_copy(hbm[k], vm[k], in_sem.at[k]) for k in range(19)}

    for k in order[:4]:
        loads[k].start()

    zs = [lax.rem(z + d, 4) for d in range(4)]
    cs = [lax.rem(core + d, 2) for d in range(2)]
    ys = [lax.rem(y + d, 4) for d in range(4)]
    xs = [lax.rem(x + d, 4) for d in range(4)]
    peers = []
    for dz, dc, dy, dx in STEPS:
        px, py = zs[dz] * 2 + cs[dc], ys[dy] * 4 + xs[dx]
        peers.append((px, py, px * NGY + py))
    barrier = pltpu.get_barrier_semaphore()
    for px, py, _ in peers:
        pl.semaphore_signal(barrier, inc=1, device_id=(px, py), device_id_type=MESH)
    for k in order[4:]:
        loads[k].start()

    def remote(src, dst, send, recv, where):
        return pltpu.make_async_remote_copy(
            src_ref=src, dst_ref=dst, send_sem=send, recv_sem=recv,
            device_id=where, device_id_type=MESH,
        )

    def to_all(src, dst, n, k, same):
        for px, py, p in peers:
            remote(
                src if same else src.at[pl.ds(p * n, n)],
                dst.at[pl.ds(me * n, n)], send_sem.at[k], recv_sem.at[k], (px, py),
            ).start()
        own = pltpu.make_async_copy(
            src if same else src.at[pl.ds(me * n, n)], dst.at[pl.ds(me * n, n)], own_sem.at[k]
        )
        own.start()

        def arrived():
            part = dst.at[pl.ds(0, (DEV - 1) * n)]
            pltpu.make_async_copy(part, part, recv_sem.at[k]).wait()
            own.wait()

        def sent():
            part = dst.at[pl.ds(0, (DEV - 1) * n)]
            pltpu.make_async_copy(part, part, send_sem.at[k]).wait()

        return arrived, sent

    for k in (6, 7, 0, 1):
        loads[k].wait()
    level_table = jnp.concatenate(split2(bed[...] + water[...]), 0)

    def bank_cells(i):
        base = pl.multiple_of(i * G, G)
        at = [pl.ds(base + j, 1) for j in range(G)]
        return base, [bank_row[a, :] for a in at], [bank_col[a, :] for a in at]

    def gather_bank(i, c):
        base, rows, cols = bank_cells(i)
        level_send[pl.ds(base, G), :] = jnp.concatenate(
            gather_chunk(level_table, rows, [one_hot(q, CY) for q in cols]), 0
        )
        return c

    lax.fori_loop(0, ROWS // G, gather_bank, 0)

    for k in (2, 3, 4, 5, 14):
        loads[k].wait()
    planes = (water, east, south, bed, rough, wet)
    lane = lax.broadcasted_iota(i32, (CX, 128), 1)
    pack_east = jnp.zeros((CX, 128), f32)
    pack_west = jnp.zeros((CX, 128), f32)
    for f, ref in enumerate(planes):
        halo_up[f] = ref[0:8, :].astype(f32)
        halo_down[f] = ref[CX - 8 : CX, :].astype(f32)
        right, left = ref[:, CY - 128 :].astype(f32), ref[:, :128].astype(f32)
        mine = (lane >= STRIP * f) & (lane < STRIP * f + 4)
        right = pltpu.roll(right, (STRIP * f + 4) % 128, 1)
        left = pltpu.roll(left, STRIP * f, 1) if f else left
        pack_east = jnp.where(mine, right, pack_east)
        pack_west = jnp.where(mine, left, pack_west)
    strip_east[...] = pack_east
    strip_west[...] = pack_west
    old_send[...] = old[SEC - 1 : SEC, :]

    pl.semaphore_wait(barrier, DEV - 1)

    level_arrived, level_sent = to_all(level_send, level_here, 2, 0, False)

    north, south_to = lax.rem(gx + NGX - 1, NGX), lax.rem(gx + 1, NGX)
    west, east_to = lax.rem(gy + NGY - 1, NGY), lax.rem(gy + 1, NGY)
    after = lax.rem(me + 1, DEV)
    top, bottom = pl.ds(0, 8), pl.ds(CX - 8, 8)
    halos = [
        (halo_up, from_south, (north, gy)),
        (halo_down, from_north, (south_to, gy)),
        (strip_east, from_west, (gx, east_to)),
        (strip_west, from_east, (gx, west)),
        (strip_east.at[top], corners.at[0], (north, east_to)),
        (strip_east.at[bottom], corners.at[1], (south_to, east_to)),
        (strip_west.at[top], corners.at[2], (north, west)),
        (strip_west.at[bottom], corners.at[3], (south_to, west)),
        (old_send, old_before, (after // NGY, lax.rem(after, NGY))),
    ]
    halos = [
        remote(src, dst, halo_send.at[k], halo_recv.at[k], where)
        for k, (src, dst, where) in enumerate(halos)
    ]
    for copy in halos:
        copy.start()

    for k in (15, 16, 17):
        loads[k].wait()
    sub = lax.broadcasted_iota(i32, (SEC, RIV), 0)
    cour = courant[...]
    inverse = 1.0 / (0.5 + IMPLICIT_WEIGHT * cour)
    passing = jnp.where(junction[...] == 1, share[...], 1.0)
    carry = passing * (IMPLICIT_WEIGHT * cour - 0.5) * inverse
    old_weight = passing * (0.5 + (1.0 - IMPLICIT_WEIGHT) * cour) * inverse
    slope[...] = LATERAL_SCALE * cour * inverse
    fixed[...] = (0.5 - (1.0 - IMPLICIT_WEIGHT) * cour) * inverse * old[...]
    levels[5] = old_weight
    for n in range(5):
        levels[n] = carry
        carry = jnp.where(sub >= (1 << n), carry * pltpu.roll(carry, 1 << n, 0), carry)
    levels[6] = carry
    carry_send[...] = narrow(carry[SEC - 1 :])

    for k in (13, 8, 9):
        loads[k].wait()
    channel_table = jnp.concatenate(
        split2(jnp.concatenate([channel[:, :CY], channel[:, CY:]], 0)), 0
    )

    def link_cells(i):
        base = pl.multiple_of(i * G, G)
        reach = [link_reach[pl.ds(base + j, 1), :] for j in range(G)]
        rows = [link_sec[pl.ds(base + j, 1), :] + ((q >> 8) << 5) for j, q in enumerate(reach)]
        return base, rows, [q & 255 for q in reach]

    def gather_channel(i, c):
        base, rows, cols = link_cells(i)
        picks = [one_hot(q, CY) for q in cols]
        for j, pick in enumerate(picks):
            link_picks[pl.ds(pl.multiple_of((base + j) * LANES, LANES), LANES), :] = pick.T
        link_channel[pl.ds(base, G), :] = jnp.concatenate(
            gather_chunk(channel_table, rows, picks), 0
        )
        return c

    lax.fori_loop(0, ROWS // G, gather_channel, 0)

    own_carry = pltpu.make_async_copy(
        carry_send, carry_all.at[pl.ds(me * PER, PER)], own_sem.at[1]
    )
    own_carry.start()
    for dz, dc, dy, dx in STEPS:
        if dz == 0 and dc == 0:
            remote(
                carry_send, carry_all.at[pl.ds(me * PER, PER)], send_sem.at[1], recv_sem.at[1],
                (gx, ys[dy] * 4 + xs[dx]),
            ).start()

    def drain(rows, sem):
        part = carry_all.at[pl.ds(0, rows)]
        pltpu.make_async_copy(part, part, sem).wait()


    halos[8].wait_recv()
    loads[18].wait()
    previous = jnp.where(
        sub == 0,
        jnp.where(me == 0, inflow[...], old_before[...]),
        pltpu.roll(old[...], 1, 0),
    )
    fixed[...] = fixed[...] + levels[5] * previous

    for k in (10, 11, 12):
        loads[k].wait()
    level_arrived()

    def flow_part(i, c):
        at = pl.ds(pl.multiple_of(i * 32, 32), 32)
        plain, chan, top, rule = level_here[at, :], link_channel[at, :], crest[at, :], regime[at, :]
        upper = jnp.maximum(chan - top, 0.0)
        lower = jnp.maximum(plain - top, 0.0)
        free = upper * jnp.sqrt(upper) - lower * jnp.sqrt(lower)
        drop = chan - plain
        drowned = drop * jnp.sqrt(jnp.abs(drop))
        flow_send[at, :] = factor[at, :] * jnp.where(
            rule == 1, free, jnp.where(rule == 2, drowned, 0.0)
        )
        return c

    lax.fori_loop(0, 8, flow_part, 0)
    flow_arrived, flow_sent = to_all(flow_send, flow_here, 2, 2, False)

    def scatter_lateral(i, acc):
        base, rows, _ = link_cells(i)
        parts = row_parts([flow_send[pl.ds(base + j, 1), :] for j in range(G)], rows)
        picks = link_picks[pl.ds(pl.multiple_of(base * LANES, LANES), G * LANES), :]
        return acc + jnp.dot(parts, picks, preferred_element_type=f32)

    acc = lax.fori_loop(0, ROWS // G, scatter_lateral, jnp.zeros((128, CY), f32))
    acc = acc[:64] + acc[64:]
    lateral = jnp.concatenate([acc[:SEC], acc[SEC:]], 1)

    own_carry.wait()
    drain((NGY - 1) * PER, recv_sem.at[1])
    block = carry_all.at[pl.ds(gx * (NGY * PER), NGY * PER)]
    for dz, dc, dy, dx in STEPS:
        if dy == 0 and dx == 0:
            remote(
                block, block, send_sem.at[4], recv_sem.at[4], (zs[dz] * 2 + cs[dc], gy)
            ).start()

    shift = fixed[...] - slope[...] * lateral
    for n in range(5):
        shift = jnp.where(
            sub >= (1 << n), levels[n] * pltpu.roll(shift, 1 << n, 0) + shift, shift
        )
    fixed[...] = shift
    shift_send[...] = narrow(shift[SEC - 1 :])
    shift_arrived, shift_sent = to_all(shift_send, shift_all, PER, 3, True)

    for copy in halos[:8]:
        copy.wait_recv()
    sub8 = lax.broadcasted_iota(i32, (8, CY), 0)
    held = []
    lanes = lax.broadcasted_iota(i32, (PX, 128), 1)
    side = lax.broadcasted_iota(i32, (PX, 128), 0)
    low, high = gx < NGX - 1, gx > 0
    edge8 = lax.broadcasted_iota(i32, (8, 128), 0)
    rows_in = (side < CX) | ((side < CX + 4) & low) | ((side >= CX + 4) & high)
    strip_left = jnp.concatenate(
        [from_west[...], jnp.where(edge8 < 4, corners[0], corners[1])], 0
    )
    strip_right = jnp.concatenate(
        [from_east[...], jnp.where(edge8 < 4, corners[2], corners[3])], 0
    )
    strip_left = jnp.where(rows_in & (gy > 0), strip_left, 0.0)
    strip_right = jnp.where(rows_in & (gy < NGY - 1), strip_right, 0.0)
    for f, ref in enumerate(planes):
        beyond = jnp.where(
            sub8 < 4, jnp.where(low, from_south[f], 0.0), jnp.where(high, from_north[f], 0.0)
        )
        fields[f, 0:CX, 0:CY] = ref[...].astype(f32)
        fields[f, CX:PX, 0:CY] = beyond
        right = pltpu.roll(strip_right, (128 - STRIP * f) % 128, 1) if f else strip_right
        left = pltpu.roll(strip_left, (128 - STRIP * f - 4) % 128, 1)
        fields[f, :, CY:PY] = jnp.where(
            lanes < 4, right, jnp.where(lanes >= 124, left, 0.0)
        )
        held.append(fields[f])
    depth, q_east, q_south, ground, manning, wetness = held

    def of_east(a):
        return pltpu.roll(a, PY - 1, 1)

    def of_south(a):
        return pltpu.roll(a, PX - 1, 0)

    faces = []
    for move in (of_east, of_south):
        mean = 0.5 * (manning + move(manning))
        faces.append(
            (
                move,
                jnp.maximum(ground, move(ground)),
                GRAVITY * TIME_STEP * mean * mean,
                wetness * move(wetness),
            )
        )
    flux = [q_east, q_south]
    for _ in range(SUBSTEPS):
        surface = ground + depth
        for n, (move, top, rub, open_) in enumerate(faces):
            beside = move(surface)
            flow_depth = jnp.maximum(jnp.maximum(surface, beside) - top, MIN_FLOW_DEPTH)
            drive = flux[n] - (GRAVITY * TIME_STEP / SPACING) * flow_depth * (beside - surface)
            friction = 1.0 + rub * jnp.abs(flux[n]) * jnp.exp((-7.0 / 3.0) * jnp.log(flow_depth))
            flux[n] = open_ * drive / friction
        depth = depth + (TIME_STEP / SPACING) * (
            pltpu.roll(flux[0], 1, 1) - flux[0] + pltpu.roll(flux[1], 1, 0) - flux[1]
        )
    east_out[...] = flux[0][:CX, :CY]
    south_out[...] = flux[1][:CX, :CY]
    fields[0] = depth

    flow_arrived()

    def scatter_bank(i, acc):
        base, rows, cols = bank_cells(i)
        return acc + scatter_chunk(
            [flow_here[pl.ds(base + j, 1), :] for j in range(G)], rows, cols
        )

    acc = lax.fori_loop(0, ROWS // G, scatter_bank, jnp.zeros((CY, 128), f32)).T
    depth_out[...] = fields[0, 0:CX, 0:CY] + BANK_GAIN * (acc[:64] + acc[64:])

    drain((NGX - 1) * NGY * PER, recv_sem.at[4])
    half = lax.broadcasted_iota(i32, (8, LANES), 0)
    run = jnp.ones((8, LANES), f32)
    for k in range(DEV // 2 - 1, -1, -1):
        upstream = (half // PER + 2 * k) < me
        both = jnp.where(upstream, carry_all[8 * k : 8 * k + 8, :], 1.0)
        swapped = pltpu.roll(both, 4, 0)
        weight = jnp.where(half < PER, swapped, 1.0) * run
        weights[8 * k : 8 * k + 8, :] = jnp.where(upstream, weight, 0.0)
        run = run * (both * swapped)
    start = wide(run[:PER]) * inflow[...]

    shift_arrived()
    parts = [
        weights[8 * k : 8 * k + 8, :] * shift_all[8 * k : 8 * k + 8, :] for k in range(DEV // 2)
    ]
    while len(parts) > 1:
        parts = [u + v for u, v in zip(parts[::2], parts[1::2])]
    enters = start + wide(parts[0][:PER] + parts[0][PER:])
    river_out[...] = levels[6] * enters + fixed[...]

    for sent in (level_sent, flow_sent, shift_sent):
        sent()
    drain((NGY - 1) * PER, send_sem.at[1])
    drain((NGX - 1) * NGY * PER, send_sem.at[4])
    for copy in halos:
        copy.wait_send()


def write_out(*refs):
    copies = [pltpu.make_async_copy(refs[k], refs[4 + k], refs[8].at[k]) for k in range(4)]
    for copy in copies:
        copy.start()
    for copy in copies:
        copy.wait()


def on_device(*args):
    args = list(args)
    for k in range(6, 13):
        args[k] = args[k].reshape(ROWS, 128)
    args[18] = args[18].reshape(1, RIV)
    vmem = lambda *shape: pltpu.VMEM(shape, f32)
    dma = pltpu.SemaphoreType.DMA
    scratch = [pltpu.VMEM(a.shape, a.dtype) for a in args]
    scratch += [vmem(ROWS, 128)] * 5
    scratch += [vmem(6, 8, CY)] * 4
    scratch += [vmem(CX, 128)] * 4 + [vmem(4, 8, 128)]
    scratch += [vmem(1, RIV)] * 2
    scratch += [vmem(PER, LANES), vmem(DEV * PER, LANES)] * 2 + [vmem(DEV * PER, LANES)]
    scratch += [vmem(6, PX, PY), vmem(7, SEC, RIV), vmem(SEC, RIV), vmem(SEC, RIV)]
    scratch += [pltpu.VMEM((ROWS * LANES, CY), bf16)]
    scratch += [dma((19,)), dma((4,)), dma((5,)), dma((5,)), dma((9,)), dma((9,))]
    results = pl.pallas_call(
        kernel,
        out_shape=(vmem(CX, CY), vmem(CX, CY), vmem(CX, CY), vmem(SEC, RIV)),
        in_specs=[pl.BlockSpec(memory_space=pl.ANY)] * 19,
        out_specs=[pl.BlockSpec(memory_space=pltpu.VMEM)] * 4,
        scratch_shapes=scratch,
        compiler_params=pltpu.CompilerParams(
            collective_id=0, has_side_effects=True, vmem_limit_bytes=62 << 20
        ),
        cost_estimate=pl.CostEstimate(
            flops=8 * 10**9, bytes_accessed=2 * 10**6, transcendentals=10**6
        ),
        name="coupled_step",
    )(*args)
    return pl.pallas_call(
        write_out,
        out_shape=[jax.ShapeDtypeStruct(r.shape, f32) for r in results],
        in_specs=[pl.BlockSpec(memory_space=pltpu.VMEM)] * 4,
        out_specs=[pl.BlockSpec(memory_space=pl.ANY)] * 4,
        scratch_shapes=[dma((4,))],
        name="write_out",
    )(*[pltpu.with_memory_space_constraint(r, pltpu.VMEM) for r in results])


def solution(mesh):
    tile, flat, chain = P("gx", "gy"), P(("gx", "gy")), P(("gx", "gy"), None)
    in_specs = (tile,) * 6 + (flat,) * 7 + (chain,) * 5 + (P(),)
    out_specs = (tile, tile, tile, chain)
    return jax.shard_map(
        on_device, mesh=mesh, in_specs=in_specs, out_specs=out_specs, check_vma=False
    )
```

```python
import functools

import jax
import jax.numpy as jnp
from jax import lax
from jax.experimental import pallas as pl
from jax.experimental.pallas import tpu as pltpu
from jax.sharding import PartitionSpec as P

GRAVITY = 9.81
SPACING = 20.0
TIME_STEP = 2.2
MIN_FLOW_DEPTH = 0.3
IMPLICIT_WEIGHT = 0.6
LATERAL_SCALE = 0.01
BANK_GAIN = 0.5
SUBSTEPS = 4

f32, bf16, i32, i16 = jnp.float32, jnp.bfloat16, jnp.int32, jnp.int16
MESH = pl.DeviceIdType.MESH

NGX, NGY = 8, 16
CX, CY = 64, 256
SEC, RIV = 32, 512
ROWS = 256
G = 128
DEV = NGX * NGY
PX, PY = CX + 8, CY + 128
STRIP = 8
LANES = 128
PER = RIV // LANES


def far_first():
    steps = [
        (z, c, y, x) for z in range(4) for c in range(2) for y in range(4) for x in range(4)
    ][1:]
    far = lambda s: min(s[0], 4 - s[0]) + min(s[2], 4 - s[2]) + min(s[3], 4 - s[3]) + 0.3 * s[1]
    return sorted(steps, key=far, reverse=True)


STEPS = far_first()


def split2(x):
    hi = x.astype(bf16)
    return hi, (x - hi.astype(f32)).astype(bf16)


def one_hot(index_row, width):
    iota = lax.broadcasted_iota(i16, (width, 128), 0)
    index = jnp.broadcast_to(index_row.astype(i16), (width, 128))
    return jnp.where(iota == index, jnp.ones((), bf16), jnp.zeros((), bf16))


def gather_chunk(table, rows, picks):
    iota = lax.broadcasted_iota(i32, (64, 128), 0)
    picks = jnp.concatenate(picks, 1)
    both = jnp.dot(table, picks, preferred_element_type=f32)
    both = both[:64] + both[64:]
    out = []
    for j, r in enumerate(rows):
        part = both[:, j * 128 : (j + 1) * 128]
        out.append(jnp.sum(jnp.where(iota == r, part, 0.0), 0, keepdims=True))
    return out


def row_parts(flows, rows):
    iota = lax.broadcasted_iota(i16, (64, 128), 0)
    zero = jnp.zeros((), bf16)
    parts = []
    for flow, r in zip(flows, rows):
        mask = iota == jnp.broadcast_to(r.astype(i16), (64, 128))
        parts.append(
            jnp.concatenate(
                [jnp.where(mask, jnp.broadcast_to(p, (64, 128)), zero) for p in split2(flow)], 0
            )
        )
    return jnp.concatenate(parts, 1)


def scatter_chunk(flows, rows, cols):
    picks = jnp.concatenate([one_hot(c, 256) for c in cols], 1)
    return lax.dot_general(
        picks, row_parts(flows, rows), (((1,), (1,)), ((), ())), preferred_element_type=f32
    )


def wide(x):
    return jnp.concatenate([x[q : q + 1] for q in range(PER)], 1)


def narrow(x):
    return jnp.concatenate([x[:, q * LANES : (q + 1) * LANES] for q in range(PER)], 0)


def kernel(*refs):
    hbm = refs[:19]
    depth_out, east_out, south_out, river_out = refs[19:23]
    vm = refs[23:42]
    (
        level_send, level_here, link_channel, flow_send, flow_here,
        halo_up, halo_down, from_north, from_south,
        strip_east, strip_west, from_west, from_east, corners,
        old_send, old_before, carry_send, carry_all, shift_send, shift_all, weights,
        fields, levels, fixed, slope, link_picks,
        in_sem, own_sem, send_sem, recv_sem, halo_send, halo_recv,
    ) = refs[42:]
    (
        water, bed, rough, wet, east, south, bank_row, bank_col, link_sec, link_reach,
        crest, factor, regime, channel, old, courant, junction, share, inflow,
    ) = vm

    gx, gy = lax.axis_index("gx"), lax.axis_index("gy")
    me = gx * NGY + gy
    z, core, y, x = gx // 2, lax.rem(gx, 2), gy // 4, lax.rem(gy, 4)

    order = [6, 7, 0, 1, 2, 3, 4, 5, 15, 16, 17, 14, 13, 8, 9, 10, 11, 12, 18]
    loads = {k: pltpu.make_async_copy(hbm[k], vm[k], in_sem.at[k]) for k in range(19)}

    for k in order[:4]:
        loads[k].start()

    zs = [lax.rem(z + d, 4) for d in range(4)]
    cs = [lax.rem(core + d, 2) for d in range(2)]
    ys = [lax.rem(y + d, 4) for d in range(4)]
    xs = [lax.rem(x + d, 4) for d in range(4)]
    peers = []
    for dz, dc, dy, dx in STEPS:
        px, py = zs[dz] * 2 + cs[dc], ys[dy] * 4 + xs[dx]
        peers.append((px, py, px * NGY + py))
    barrier = pltpu.get_barrier_semaphore()
    for px, py, _ in peers:
        pl.semaphore_signal(barrier, inc=1, device_id=(px, py), device_id_type=MESH)
    for k in order[4:]:
        loads[k].start()

    def remote(src, dst, send, recv, where):
        return pltpu.make_async_remote_copy(
            src_ref=src, dst_ref=dst, send_sem=send, recv_sem=recv,
            device_id=where, device_id_type=MESH,
        )

    def to_all(src, dst, n, k, same):
        for px, py, p in peers:
            remote(
                src if same else src.at[pl.ds(p * n, n)],
                dst.at[pl.ds(me * n, n)], send_sem.at[k], recv_sem.at[k], (px, py),
            ).start()
        own = pltpu.make_async_copy(
            src if same else src.at[pl.ds(me * n, n)], dst.at[pl.ds(me * n, n)], own_sem.at[k]
        )
        own.start()

        def arrived():
            part = dst.at[pl.ds(0, (DEV - 1) * n)]
            pltpu.make_async_copy(part, part, recv_sem.at[k]).wait()
            own.wait()

        def sent():
            part = dst.at[pl.ds(0, (DEV - 1) * n)]
            pltpu.make_async_copy(part, part, send_sem.at[k]).wait()

        return arrived, sent

    for k in (6, 7, 0, 1):
        loads[k].wait()
    level_table = jnp.concatenate(split2(bed[...] + water[...]), 0)

    def bank_cells(i):
        base = pl.multiple_of(i * G, G)
        at = [pl.ds(base + j, 1) for j in range(G)]
        return base, [bank_row[a, :] for a in at], [bank_col[a, :] for a in at]

    def gather_bank(i, c):
        base, rows, cols = bank_cells(i)
        level_send[pl.ds(base, G), :] = jnp.concatenate(
            gather_chunk(level_table, rows, [one_hot(q, CY) for q in cols]), 0
        )
        return c

    lax.fori_loop(0, ROWS // G, gather_bank, 0)

    pl.semaphore_wait(barrier, DEV - 1)

    level_arrived, level_sent = to_all(level_send, level_here, 2, 0, False)

    for k in (2, 3, 4, 5, 14):
        loads[k].wait()
    planes = (water, east, south, bed, rough, wet)
    lane = lax.broadcasted_iota(i32, (CX, 128), 1)
    pack_east = jnp.zeros((CX, 128), f32)
    pack_west = jnp.zeros((CX, 128), f32)
    for f, ref in enumerate(planes):
        halo_up[f] = ref[0:8, :].astype(f32)
        halo_down[f] = ref[CX - 8 : CX, :].astype(f32)
        right, left = ref[:, CY - 128 :].astype(f32), ref[:, :128].astype(f32)
        mine = (lane >= STRIP * f) & (lane < STRIP * f + 4)
        right = pltpu.roll(right, (STRIP * f + 4) % 128, 1)
        left = pltpu.roll(left, STRIP * f, 1) if f else left
        pack_east = jnp.where(mine, right, pack_east)
        pack_west = jnp.where(mine, left, pack_west)
    strip_east[...] = pack_east
    strip_west[...] = pack_west
    old_send[...] = old[SEC - 1 : SEC, :]


    north, south_to = lax.rem(gx + NGX - 1, NGX), lax.rem(gx + 1, NGX)
    west, east_to = lax.rem(gy + NGY - 1, NGY), lax.rem(gy + 1, NGY)
    after = lax.rem(me + 1, DEV)
    top, bottom = pl.ds(0, 8), pl.ds(CX - 8, 8)
    halos = [
        (halo_up, from_south, (north, gy)),
        (halo_down, from_north, (south_to, gy)),
        (strip_east, from_west, (gx, east_to)),
        (strip_west, from_east, (gx, west)),
        (strip_east.at[top], corners.at[0], (north, east_to)),
        (strip_east.at[bottom], corners.at[1], (south_to, east_to)),
        (strip_west.at[top], corners.at[2], (north, west)),
        (strip_west.at[bottom], corners.at[3], (south_to, west)),
        (old_send, old_before, (after // NGY, lax.rem(after, NGY))),
    ]
    halos = [
        remote(src, dst, halo_send.at[k], halo_recv.at[k], where)
        for k, (src, dst, where) in enumerate(halos)
    ]
    for copy in halos:
        copy.start()

    for k in (15, 16, 17):
        loads[k].wait()
    sub = lax.broadcasted_iota(i32, (SEC, RIV), 0)
    cour = courant[...]
    inverse = 1.0 / (0.5 + IMPLICIT_WEIGHT * cour)
    passing = jnp.where(junction[...] == 1, share[...], 1.0)
    carry = passing * (IMPLICIT_WEIGHT * cour - 0.5) * inverse
    old_weight = passing * (0.5 + (1.0 - IMPLICIT_WEIGHT) * cour) * inverse
    slope[...] = LATERAL_SCALE * cour * inverse
    fixed[...] = (0.5 - (1.0 - IMPLICIT_WEIGHT) * cour) * inverse * old[...]
    levels[5] = old_weight
    for n in range(5):
        levels[n] = carry
        carry = jnp.where(sub >= (1 << n), carry * pltpu.roll(carry, 1 << n, 0), carry)
    levels[6] = carry
    carry_send[...] = narrow(carry[SEC - 1 :])

    for k in (13, 8, 9):
        loads[k].wait()
    channel_table = jnp.concatenate(
        split2(jnp.concatenate([channel[:, :CY], channel[:, CY:]], 0)), 0
    )

    def link_cells(i):
        base = pl.multiple_of(i * G, G)
        reach = [link_reach[pl.ds(base + j, 1), :] for j in range(G)]
        rows = [link_sec[pl.ds(base + j, 1), :] + ((q >> 8) << 5) for j, q in enumerate(reach)]
        return base, rows, [q & 255 for q in reach]

    def gather_channel(i, c):
        base, rows, cols = link_cells(i)
        picks = [one_hot(q, CY) for q in cols]
        for j, pick in enumerate(picks):
            link_picks[pl.ds(pl.multiple_of((base + j) * LANES, LANES), LANES), :] = pick.T
        link_channel[pl.ds(base, G), :] = jnp.concatenate(
            gather_chunk(channel_table, rows, picks), 0
        )
        return c

    lax.fori_loop(0, ROWS // G, gather_channel, 0)

    own_carry = pltpu.make_async_copy(
        carry_send, carry_all.at[pl.ds(me * PER, PER)], own_sem.at[1]
    )
    own_carry.start()
    for dz, dc, dy, dx in STEPS:
        if dz == 0 and dc == 0:
            remote(
                carry_send, carry_all.at[pl.ds(me * PER, PER)], send_sem.at[1], recv_sem.at[1],
                (gx, ys[dy] * 4 + xs[dx]),
            ).start()

    def drain(rows, sem):
        part = carry_all.at[pl.ds(0, rows)]
        pltpu.make_async_copy(part, part, sem).wait()


    halos[8].wait_recv()
    loads[18].wait()
    previous = jnp.where(
        sub == 0,
        jnp.where(me == 0, inflow[...], old_before[...]),
        pltpu.roll(old[...], 1, 0),
    )
    fixed[...] = fixed[...] + levels[5] * previous

    for k in (10, 11, 12):
        loads[k].wait()
    level_arrived()

    def flow_part(i, c):
        at = pl.ds(pl.multiple_of(i * 32, 32), 32)
        plain, chan, top, rule = level_here[at, :], link_channel[at, :], crest[at, :], regime[at, :]
        upper = jnp.maximum(chan - top, 0.0)
        lower = jnp.maximum(plain - top, 0.0)
        free = upper * jnp.sqrt(upper) - lower * jnp.sqrt(lower)
        drop = chan - plain
        drowned = drop * jnp.sqrt(jnp.abs(drop))
        flow_send[at, :] = factor[at, :] * jnp.where(
            rule == 1, free, jnp.where(rule == 2, drowned, 0.0)
        )
        return c

    lax.fori_loop(0, 8, flow_part, 0)
    flow_arrived, flow_sent = to_all(flow_send, flow_here, 2, 2, False)

    def scatter_lateral(i, acc):
        base, rows, _ = link_cells(i)
        parts = row_parts([flow_send[pl.ds(base + j, 1), :] for j in range(G)], rows)
        picks = link_picks[pl.ds(pl.multiple_of(base * LANES, LANES), G * LANES), :]
        return acc + jnp.dot(parts, picks, preferred_element_type=f32)

    acc = lax.fori_loop(0, ROWS // G, scatter_lateral, jnp.zeros((128, CY), f32))
    acc = acc[:64] + acc[64:]
    lateral = jnp.concatenate([acc[:SEC], acc[SEC:]], 1)

    own_carry.wait()
    drain((NGY - 1) * PER, recv_sem.at[1])
    block = carry_all.at[pl.ds(gx * (NGY * PER), NGY * PER)]
    for dz, dc, dy, dx in STEPS:
        if dy == 0 and dx == 0:
            remote(
                block, block, send_sem.at[4], recv_sem.at[4], (zs[dz] * 2 + cs[dc], gy)
            ).start()

    shift = fixed[...] - slope[...] * lateral
    for n in range(5):
        shift = jnp.where(
            sub >= (1 << n), levels[n] * pltpu.roll(shift, 1 << n, 0) + shift, shift
        )
    fixed[...] = shift
    shift_send[...] = narrow(shift[SEC - 1 :])
    shift_arrived, shift_sent = to_all(shift_send, shift_all, PER, 3, True)

    for copy in halos[:8]:
        copy.wait_recv()
    sub8 = lax.broadcasted_iota(i32, (8, CY), 0)
    held = []
    lanes = lax.broadcasted_iota(i32, (PX, 128), 1)
    side = lax.broadcasted_iota(i32, (PX, 128), 0)
    low, high = gx < NGX - 1, gx > 0
    edge8 = lax.broadcasted_iota(i32, (8, 128), 0)
    rows_in = (side < CX) | ((side < CX + 4) & low) | ((side >= CX + 4) & high)
    strip_left = jnp.concatenate(
        [from_west[...], jnp.where(edge8 < 4, corners[0], corners[1])], 0
    )
    strip_right = jnp.concatenate(
        [from_east[...], jnp.where(edge8 < 4, corners[2], corners[3])], 0
    )
    strip_left = jnp.where(rows_in & (gy > 0), strip_left, 0.0)
    strip_right = jnp.where(rows_in & (gy < NGY - 1), strip_right, 0.0)
    for f, ref in enumerate(planes):
        beyond = jnp.where(
            sub8 < 4, jnp.where(low, from_south[f], 0.0), jnp.where(high, from_north[f], 0.0)
        )
        fields[f, 0:CX, 0:CY] = ref[...].astype(f32)
        fields[f, CX:PX, 0:CY] = beyond
        right = pltpu.roll(strip_right, (128 - STRIP * f) % 128, 1) if f else strip_right
        left = pltpu.roll(strip_left, (128 - STRIP * f - 4) % 128, 1)
        fields[f, :, CY:PY] = jnp.where(
            lanes < 4, right, jnp.where(lanes >= 124, left, 0.0)
        )
        held.append(fields[f])
    depth, q_east, q_south, ground, manning, wetness = held

    def of_east(a):
        return pltpu.roll(a, PY - 1, 1)

    def of_south(a):
        return pltpu.roll(a, PX - 1, 0)

    faces = []
    for move in (of_east, of_south):
        mean = 0.5 * (manning + move(manning))
        faces.append(
            (
                move,
                jnp.maximum(ground, move(ground)),
                GRAVITY * TIME_STEP * mean * mean,
                wetness * move(wetness),
            )
        )
    flux = [q_east, q_south]
    for _ in range(SUBSTEPS):
        surface = ground + depth
        for n, (move, top, rub, open_) in enumerate(faces):
            beside = move(surface)
            flow_depth = jnp.maximum(jnp.maximum(surface, beside) - top, MIN_FLOW_DEPTH)
            drive = flux[n] - (GRAVITY * TIME_STEP / SPACING) * flow_depth * (beside - surface)
            friction = 1.0 + rub * jnp.abs(flux[n]) * jnp.exp((-7.0 / 3.0) * jnp.log(flow_depth))
            flux[n] = open_ * drive / friction
        depth = depth + (TIME_STEP / SPACING) * (
            pltpu.roll(flux[0], 1, 1) - flux[0] + pltpu.roll(flux[1], 1, 0) - flux[1]
        )
    east_out[...] = flux[0][:CX, :CY]
    south_out[...] = flux[1][:CX, :CY]
    fields[0] = depth

    flow_arrived()

    def scatter_bank(i, acc):
        base, rows, cols = bank_cells(i)
        return acc + scatter_chunk(
            [flow_here[pl.ds(base + j, 1), :] for j in range(G)], rows, cols
        )

    acc = lax.fori_loop(0, ROWS // G, scatter_bank, jnp.zeros((CY, 128), f32)).T
    depth_out[...] = fields[0, 0:CX, 0:CY] + BANK_GAIN * (acc[:64] + acc[64:])

    drain((NGX - 1) * NGY * PER, recv_sem.at[4])
    half = lax.broadcasted_iota(i32, (8, LANES), 0)
    run = jnp.ones((8, LANES), f32)
    for k in range(DEV // 2 - 1, -1, -1):
        upstream = (half // PER + 2 * k) < me
        both = jnp.where(upstream, carry_all[8 * k : 8 * k + 8, :], 1.0)
        swapped = pltpu.roll(both, 4, 0)
        weight = jnp.where(half < PER, swapped, 1.0) * run
        weights[8 * k : 8 * k + 8, :] = jnp.where(upstream, weight, 0.0)
        run = run * (both * swapped)
    start = wide(run[:PER]) * inflow[...]

    shift_arrived()
    parts = [
        weights[8 * k : 8 * k + 8, :] * shift_all[8 * k : 8 * k + 8, :] for k in range(DEV // 2)
    ]
    while len(parts) > 1:
        parts = [u + v for u, v in zip(parts[::2], parts[1::2])]
    enters = start + wide(parts[0][:PER] + parts[0][PER:])
    river_out[...] = levels[6] * enters + fixed[...]

    for sent in (level_sent, flow_sent, shift_sent):
        sent()
    drain((NGY - 1) * PER, send_sem.at[1])
    drain((NGX - 1) * NGY * PER, send_sem.at[4])
    for copy in halos:
        copy.wait_send()


def write_out(*refs):
    copies = [pltpu.make_async_copy(refs[k], refs[4 + k], refs[8].at[k]) for k in range(4)]
    for copy in copies:
        copy.start()
    for copy in copies:
        copy.wait()


def on_device(*args):
    args = list(args)
    for k in range(6, 13):
        args[k] = args[k].reshape(ROWS, 128)
    args[18] = args[18].reshape(1, RIV)
    vmem = lambda *shape: pltpu.VMEM(shape, f32)
    dma = pltpu.SemaphoreType.DMA
    scratch = [pltpu.VMEM(a.shape, a.dtype) for a in args]
    scratch += [vmem(ROWS, 128)] * 5
    scratch += [vmem(6, 8, CY)] * 4
    scratch += [vmem(CX, 128)] * 4 + [vmem(4, 8, 128)]
    scratch += [vmem(1, RIV)] * 2
    scratch += [vmem(PER, LANES), vmem(DEV * PER, LANES)] * 2 + [vmem(DEV * PER, LANES)]
    scratch += [vmem(6, PX, PY), vmem(7, SEC, RIV), vmem(SEC, RIV), vmem(SEC, RIV)]
    scratch += [pltpu.VMEM((ROWS * LANES, CY), bf16)]
    scratch += [dma((19,)), dma((4,)), dma((5,)), dma((5,)), dma((9,)), dma((9,))]
    results = pl.pallas_call(
        kernel,
        out_shape=(vmem(CX, CY), vmem(CX, CY), vmem(CX, CY), vmem(SEC, RIV)),
        in_specs=[pl.BlockSpec(memory_space=pl.ANY)] * 19,
        out_specs=[pl.BlockSpec(memory_space=pltpu.VMEM)] * 4,
        scratch_shapes=scratch,
        compiler_params=pltpu.CompilerParams(
            collective_id=0, has_side_effects=True, vmem_limit_bytes=62 << 20
        ),
        cost_estimate=pl.CostEstimate(
            flops=8 * 10**9, bytes_accessed=2 * 10**6, transcendentals=10**6
        ),
        name="coupled_step",
    )(*args)
    return pl.pallas_call(
        write_out,
        out_shape=[jax.ShapeDtypeStruct(r.shape, f32) for r in results],
        in_specs=[pl.BlockSpec(memory_space=pltpu.VMEM)] * 4,
        out_specs=[pl.BlockSpec(memory_space=pl.ANY)] * 4,
        scratch_shapes=[dma((4,))],
        name="write_out",
    )(*[pltpu.with_memory_space_constraint(r, pltpu.VMEM) for r in results])


def solution(mesh):
    tile, flat, chain = P("gx", "gy"), P(("gx", "gy")), P(("gx", "gy"), None)
    in_specs = (tile,) * 6 + (flat,) * 7 + (chain,) * 5 + (P(),)
    out_specs = (tile, tile, tile, chain)
    return jax.shard_map(
        on_device, mesh=mesh, in_specs=in_specs, out_specs=out_specs, check_vma=False
    )
```
